128 devices in a mesh: context: 16 (over y, z), seq: 4 (over x), tensor: 2 (over core).
Axes of the slice: x: 4, y: 4, z: 4, core: 2. Of those that a mesh axis runs over, the one named last changes fastest.
Arguments:
- queries: bfloat16 [16384, 2048], P(('seq', 'context'), 'tensor'), parts along dimension 0, may hold values from -9 to 9
- key_states: bfloat16 [16384, 512], P(('seq', 'context'), 'tensor'), parts along dimension 0, may hold values from -4 to 4
- value_states: bfloat16 [16384, 512], P(('seq', 'context'), 'tensor'), parts along dimension 0, may hold values from -6 to 6
- segment_ids: int32 [16384], P('seq'), parts along dimension 0, may hold values from 0 to 3, never falling along the last dimension, each value on 1 to 3072 neighbouring positions
- hidden: bfloat16 [16384, 2048], P(('seq', 'context')), parts along dimension 0, may hold values from -6 to 6
- attn_out_weight: bfloat16 [2048, 2048], P('tensor'), may hold values from -0.125 to 0.125
- norm_gain: bfloat16 [2048], replicated, may hold values from 0.5 to 1.5
- gate_weight: bfloat16 [2048, 4096], P(None, 'tensor'), may hold values from -0.125 to 0.125
- inner_weight: bfloat16 [2048, 4096], P(None, 'tensor'), may hold values from -0.125 to 0.125
- state_proj_weight: bfloat16 [2048, 256], replicated, may hold values from -0.125 to 0.125
- step_weight: bfloat16 [2048, 64], P(None, 'tensor'), may hold values from -0.125 to 0.125
- conv_inner: bfloat16 [4, 4096], P(None, 'tensor'), may hold values from -3 to 3
- conv_state: bfloat16 [4, 256], replicated, may hold values from -3 to 3
- step_bias: float32 [64], P('tensor'), may hold values from -4 to 0
- decay_log: float32 [64], P('tensor'), may hold values from -12 to 3
- skip_gain: float32 [64], P('tensor'), may hold values from 0.5 to 1.5
- out_gain: bfloat16 [4096], P('tensor'), may hold values from 0.5 to 1.5
Outputs:
- residual: bfloat16 [16384, 2048], P(('seq', 'context')), parts along dimension 0
- mixed: bfloat16 [16384, 4096], P(('seq', 'context'), 'tensor'), parts along dimension 0
The draws below stay inside these ranges and needn't reach their ends.
There are 4 independent parts, one for each index of `seq`. The reference program is written for one: setup_inputs(seed, part) draws one part's arguments, and reference() takes and returns one part's arrays. A program takes and returns all parts, laid end to end along the dimension named above; an argument that names none is the same for every part. Nothing has to cross between parts.
Inputs may be any that keep to these rules, and one draw needn't show every extreme that they name: `segment_ids`: segment ids never fall along a sequence.
All inputs are finite; a program needn't handle non-finite values.
Results may differ from the reference program's by a relative error of at most 0.012.
Values may be sent and summed in bfloat16 or wider, within the bound.
No kernel may reach another device: no remote copies, remote signals or barrier semaphores. Data moves between devices by JAX's collectives and lax.ppermute only.
A program may use at most 128 MiB of HBM per device.

```python
import math
import jax
import jax.numpy as jnp
import numpy as np
from jax import lax

D = 2048
ATT_HEADS = 16
KV_HEADS = 4
HEAD_DIM = 128
SSM_HEADS = 64
SSM_HEAD_DIM = 64
STATE = 128
CONV = 4
WINDOW = 2048
SEGMENTS = 4
TOK_DEV = 256
LENGTH = 4096
D_INNER = 4096


def draw_queries(key, part):
    shape = (LENGTH, ATT_HEADS * HEAD_DIM)
    base = jnp.clip(jax.random.normal(jax.random.fold_in(key, 1), shape, jnp.float32), -4.0, 4.0)
    return base.astype(jnp.bfloat16)


def draw_key_states(key, part):
    shape = (LENGTH, KV_HEADS * HEAD_DIM)
    base = jnp.clip(jax.random.normal(jax.random.fold_in(key, 2), shape, jnp.float32), -4.0, 4.0)
    return base.astype(jnp.bfloat16)


def draw_step_bias(key, part):
    return jax.random.uniform(jax.random.fold_in(key, 3), (SSM_HEADS,), jnp.float32, -4.0, 0.0)


def draw_decay_log(key, part):
    reach = jax.random.uniform(jax.random.fold_in(key, 4), (SSM_HEADS,), jnp.float32, math.log(0.3), math.log(300.0))
    return reach - math.log(LENGTH)


def levels(key, extent, split, least, largest):
    def one(position, blocks):
        draws = jax.random.uniform(jax.random.fold_in(jax.random.fold_in(key, 6), position), (blocks,), jnp.float32, least / len(split), largest / len(split))
        return jnp.repeat(jnp.exp(draws), extent[position] // blocks).reshape((-1,) + (1,) * (len(extent) - position - 1))

    level = one(*split[0])
    for cut in split[1:]:
        level = level * one(*cut)
    return level


def profile(number_of, total, bound, lean):
    loads = [(1 << 20) // math.isqrt(grade ** lean) + 1 for grade in range(2, number_of + 1)]
    surplus, given = total - bound - (number_of - 1), [1] * (number_of - 1)
    while surplus > 0:
        candidates = [i for i in range(number_of - 1) if given[i] < bound]
        whole, remaining = sum([loads[i] for i in candidates]), surplus
        for i in candidates:
            extra = min(bound - given[i], max(1, remaining * loads[i] // whole), surplus)
            given[i] = given[i] + extra
            surplus = surplus - extra
    return np.array([bound] + given)


def uneven(stream_key, amount, total, most, skew):
    if amount == 2:
        one = jax.random.randint(stream_key, (), max(1, total - most), min(most, total - 1) + 1)
        return jnp.stack([one, total - one])
    sizes = jnp.asarray(profile(amount, total, most, skew), jnp.int32)
    twos = (amount - 1) // 2
    source_of, taker = sizes[1:1 + 2 * twos:2], sizes[2:2 + 2 * twos:2]
    margin = jnp.minimum(source_of - 1, most - taker)
    moved = jax.random.randint(jax.random.fold_in(stream_key, 1), (twos,), 0, 1 << 20) % (margin + 1)
    sizes = sizes.at[1:1 + 2 * twos:2].set(source_of - moved).at[2:2 + 2 * twos:2].set(taker + moved)
    return sizes[jax.random.permutation(jax.random.fold_in(stream_key, 2), amount)]


def centred(rng, shape, width, bound, cuts=(), held_as=jnp.bfloat16):
    values = width * jax.random.normal(rng, shape, jnp.float32)
    if cuts:
        values = values * levels(rng, shape, cuts, -0.22, 0.18)
    return jnp.clip(values, -bound, bound).astype(held_as)


def setup_inputs(seed: int = 0, part: int = 0) -> dict:
    key_list = jax.random.split(jax.random.key(seed), 18)
    own_keys = jax.random.split(jax.random.fold_in(key_list[17], part), 18)
    queries = draw_queries(jax.random.fold_in(jax.random.fold_in(key_list[17], part), 71), part)
    key_states = draw_key_states(jax.random.fold_in(jax.random.fold_in(key_list[17], part), 71), part)
    value_states = centred(own_keys[2], (LENGTH, KV_HEADS * HEAD_DIM), 1.0, 6.0, ((0, 16), (1, 2)))
    segment_ids = jnp.searchsorted(jnp.cumsum(uneven(own_keys[3], SEGMENTS, LENGTH, 3 * LENGTH // 4, 0)), jnp.arange(LENGTH), side="right").astype(jnp.int32)
    hidden = centred(own_keys[4], (LENGTH, D), 1.0, 6.0, ((0, 16),))
    attn_out_weight = centred(key_list[5], (ATT_HEADS * HEAD_DIM, D), (ATT_HEADS * HEAD_DIM) ** -0.5, 0.125, ((0, 2),))
    norm_gain = jnp.clip(1.0 + 0.1 * jax.random.normal(key_list[6], (D,), jnp.float32), 0.5, 1.5).astype(jnp.bfloat16)
    gate_weight = centred(key_list[7], (D, D_INNER), D ** -0.5, 0.125, ((1, 2),))
    inner_weight = centred(key_list[8], (D, D_INNER), D ** -0.5, 0.125, ((1, 2),))
    state_proj_weight = centred(key_list[9], (D, 2 * STATE), D ** -0.5, 0.125)
    step_weight = centred(key_list[10], (D, SSM_HEADS), D ** -0.5, 0.125, ((1, 2),))
    conv_inner = centred(key_list[11], (CONV, D_INNER), CONV ** -0.5, 3.0, ((1, 2),))
    conv_state = centred(key_list[12], (CONV, 2 * STATE), CONV ** -0.5, 3.0)
    step_bias = draw_step_bias(jax.random.fold_in(key_list[17], 71), part)
    decay_log = draw_decay_log(jax.random.fold_in(key_list[17], 71), part)
    skip_gain = jnp.clip(0.5 + 1.0 * jax.random.uniform(key_list[15], (SSM_HEADS,), jnp.float32) ** levels(key_list[15], (SSM_HEADS,), ((0, 2),), -0.2, 0.2), 0.5, 1.5)
    out_gain = jnp.clip(1.0 + 0.1 * jax.random.normal(key_list[16], (D_INNER,), jnp.float32), 0.5, 1.5).astype(jnp.bfloat16)
    return dict(queries=queries, key_states=key_states, value_states=value_states, segment_ids=segment_ids, hidden=hidden, attn_out_weight=attn_out_weight, norm_gain=norm_gain, gate_weight=gate_weight, inner_weight=inner_weight, state_proj_weight=state_proj_weight, step_weight=step_weight, conv_inner=conv_inner, conv_state=conv_state, step_bias=step_bias, decay_log=decay_log, skip_gain=skip_gain, out_gain=out_gain)


EPSILON = 1e-05

def attend(query_rows, key_rows, value_rows, query_pos, key_pos, query_seg, key_seg):
    groups = ATT_HEADS // KV_HEADS
    count = query_rows.shape[0]
    local_heads = key_rows.shape[1] // HEAD_DIM
    shaped_q = query_rows.reshape(count, local_heads, groups, HEAD_DIM).astype(jnp.float32)
    shaped_k = key_rows.reshape(-1, local_heads, HEAD_DIM).astype(jnp.float32)
    shaped_v = value_rows.reshape(-1, local_heads, HEAD_DIM).astype(jnp.float32)
    scores = jnp.einsum('tgjd,sgd->gjts', shaped_q, shaped_k) * HEAD_DIM ** (-0.5)
    allowed = (key_pos[None, :] <= query_pos[:, None]) & (query_pos[:, None] - key_pos[None, :] < WINDOW)
    allowed = allowed & (key_seg[None, :] == query_seg[:, None])
    scores = jnp.where(allowed, scores, -jnp.inf)
    highest = lax.optimization_barrier(jnp.max(scores, axis=-1, keepdims=True))
    weights = jnp.exp(scores - highest)
    probs = (weights / lax.optimization_barrier(jnp.sum(weights, axis=-1, keepdims=True))).astype(jnp.bfloat16)
    blended = jnp.einsum('gjts,sgd->tgjd', probs.astype(jnp.float32), shaped_v)
    return blended.astype(jnp.bfloat16).reshape(count, -1)

def causal_conv(raw_rows, taps, seg_rows):
    count = raw_rows.shape[0] - CONV + 1
    target = seg_rows[CONV - 1:]
    total = jnp.zeros((count, raw_rows.shape[1]), jnp.float32)
    for tap in range(CONV):
        keep = (seg_rows[tap:tap + count] == target).astype(jnp.float32)
        total = total + taps[tap].astype(jnp.float32)[None, :] * raw_rows[tap:tap + count].astype(jnp.float32) * keep[:, None]
    return jax.nn.silu(total).astype(jnp.bfloat16)

def local_terms(shaped, read_in, read_out, step, rate, seg_rows):
    count = shaped.shape[0]
    running = jnp.cumsum(rate, axis=0)
    order = jnp.arange(count, dtype=jnp.int32)
    same = (seg_rows[:, None] == seg_rows[None, :]) & (order[:, None] >= order[None, :])
    gap = running.T[:, :, None] - running.T[:, None, :]
    decay = jnp.where(same[None], jnp.exp(jnp.where(same[None], gap, 0.0)), 0.0)
    pairwise = jnp.einsum('tn,sn->ts', read_out.astype(jnp.float32), read_in.astype(jnp.float32))
    mixing = (decay * pairwise[None] * step.T[:, None, :]).astype(jnp.bfloat16)
    within = jnp.einsum('hts,shp->thp', mixing.astype(jnp.float32), shaped.astype(jnp.float32))
    tail = jnp.exp(running[-1][None, :] - running) * (seg_rows == seg_rows[-1]).astype(jnp.float32)[:, None]
    weighted = ((tail * step)[:, :, None] * shaped.astype(jnp.float32)).astype(jnp.bfloat16)
    end_state = jnp.einsum('thp,tn->hpn', weighted.astype(jnp.float32), read_in.astype(jnp.float32))
    return (within, running, end_state)

def reference(queries, key_states, value_states, segment_ids, hidden, attn_out_weight, norm_gain, gate_weight, inner_weight, state_proj_weight, step_weight, conv_inner, conv_state, step_bias, decay_log, skip_gain, out_gain):
    length = hidden.shape[0]
    block = TOK_DEV
    blocks = length // block
    filler = jnp.zeros((WINDOW, key_states.shape[1]), key_states.dtype)
    padded_keys = jnp.concatenate([filler, key_states])
    padded_values = jnp.concatenate([filler, value_states])
    padded_seg = jnp.concatenate([jnp.full((WINDOW,), -1, jnp.int32), segment_ids])

    def one_block(index):
        start = (index * block).astype(jnp.int32)
        query_rows = lax.dynamic_slice_in_dim(queries, start, block, 0)
        key_rows = lax.dynamic_slice_in_dim(padded_keys, start, WINDOW + block, 0)
        value_rows = lax.dynamic_slice_in_dim(padded_values, start, WINDOW + block, 0)
        query_seg = lax.dynamic_slice_in_dim(segment_ids, start, block, 0)
        key_seg = lax.dynamic_slice_in_dim(padded_seg, start, WINDOW + block, 0)
        query_pos = start + jnp.arange(block, dtype=jnp.int32)
        key_pos = start - WINDOW + jnp.arange(WINDOW + block, dtype=jnp.int32)
        return attend(query_rows, key_rows, value_rows, query_pos, key_pos, query_seg, key_seg)
    attended = lax.map(one_block, jnp.arange(blocks, dtype=jnp.int32)).reshape(length, -1)
    projected = jnp.dot(attended, attn_out_weight, preferred_element_type=jnp.float32)
    residual = (hidden.astype(jnp.float32) + projected).astype(jnp.bfloat16)
    wide = residual.astype(jnp.float32)
    normed = (wide * lax.rsqrt(lax.optimization_barrier(jnp.mean(wide * wide, axis=-1, keepdims=True)) + EPSILON) * norm_gain.astype(jnp.float32)[None, :]).astype(jnp.bfloat16)
    gate = jnp.dot(normed, gate_weight, preferred_element_type=jnp.float32).astype(jnp.bfloat16)
    inner_raw = jnp.dot(normed, inner_weight, preferred_element_type=jnp.float32).astype(jnp.bfloat16)
    state_raw = jnp.dot(normed, state_proj_weight, preferred_element_type=jnp.float32).astype(jnp.bfloat16)
    step_raw = jnp.dot(normed, step_weight, preferred_element_type=jnp.float32)
    step = jax.nn.softplus(step_raw + step_bias[None, :])
    rate = -jnp.exp(decay_log)[None, :] * step
    conv_seg = jnp.concatenate([jnp.full((CONV - 1,), -1, jnp.int32), segment_ids])
    inner = causal_conv(jnp.concatenate([jnp.zeros((CONV - 1, inner_raw.shape[1]), jnp.bfloat16), inner_raw]), conv_inner, conv_seg)
    state_conv = causal_conv(jnp.concatenate([jnp.zeros((CONV - 1, state_raw.shape[1]), jnp.bfloat16), state_raw]), conv_state, conv_seg)
    read_in = state_conv[:, :STATE]
    read_out = state_conv[:, STATE:]
    shaped = inner.reshape(length, SSM_HEADS, SSM_HEAD_DIM)

    def ssd_block(carry, pieces):
        state, prior_seg = carry
        block_inner, block_in, block_out, block_step, block_rate, block_seg = pieces
        within, running, end_state = local_terms(block_inner, block_in, block_out, block_step, block_rate, block_seg)
        entry = jnp.exp(running) * (block_seg == prior_seg).astype(jnp.float32)[:, None]
        state_low = lax.optimization_barrier(state.astype(jnp.bfloat16)).astype(jnp.float32)
        incoming = jnp.einsum('tn,hpn->thp', block_out.astype(jnp.float32), state_low) * entry[:, :, None]
        end_decay = jnp.exp(running[-1]) * (block_seg[-1] == prior_seg).astype(jnp.float32)
        new_state = end_decay[:, None, None] * state + end_state
        return ((new_state, block_seg[-1]), within + incoming)
    pieces = (shaped.reshape(blocks, block, SSM_HEADS, SSM_HEAD_DIM), read_in.reshape(blocks, block, STATE), read_out.reshape(blocks, block, STATE), step.reshape(blocks, block, SSM_HEADS), rate.reshape(blocks, block, SSM_HEADS), segment_ids.reshape(blocks, block))
    start_state = jnp.zeros((SSM_HEADS, SSM_HEAD_DIM, STATE), jnp.float32)
    _, outputs = lax.scan(ssd_block, (start_state, jnp.int32(-1)), pieces)
    ssm_out = outputs.reshape(length, SSM_HEADS, SSM_HEAD_DIM) + skip_gain[None, :, None] * shaped.astype(jnp.float32)
    gated = ssm_out.reshape(length, -1) * jax.nn.silu(gate.astype(jnp.float32))
    squares = lax.optimization_barrier(jnp.sum(gated * gated, axis=-1))
    mixed = (gated * lax.rsqrt(squares / D_INNER + EPSILON)[:, None] * out_gain.astype(jnp.float32)[None, :]).astype(jnp.bfloat16)
    return (residual, mixed)
```

```python
import functools
import jax
import jax.numpy as jnp
from jax import lax
from jax.experimental import pallas as pl
from jax.experimental.pallas import tpu as pltpu
from jax.sharding import PartitionSpec as P

ATT_HEADS = 16
KV_HEADS = 4
HEAD_DIM = 128
STATE = 128
CONV = 4
WINDOW = 2048
D_INNER = 4096
ROWS = 256
REACH = 8
CONTEXT = 16
PIECE = 128
PIECE_ROWS = STATE + 16
EPSILON = 1e-05
NEG = -1e30
LOG2E = 1.4426950408889634


F32 = jnp.float32
BF16 = jnp.bfloat16


def shifted(x, by):
    pairs = [(i, i + by) for i in range(CONTEXT) if i + by < CONTEXT]
    return lax.ppermute(x, "context", pairs)


def swapped(x):
    return lax.ppermute(x, "tensor", [(0, 1), (1, 0)])


def vmem_call(kernel, out_shape, n_in, scratch=(), limit=40 << 20, flops=0, bytes_accessed=0, **kw):
    return pl.pallas_call(
        kernel,
        out_shape=out_shape,
        in_specs=[pl.BlockSpec(memory_space=pltpu.VMEM)] * n_in,
        out_specs=jax.tree.map(lambda _: pl.BlockSpec(memory_space=pltpu.VMEM), out_shape),
        scratch_shapes=list(scratch),
        compiler_params=pltpu.CompilerParams(vmem_limit_bytes=limit),
        cost_estimate=pl.CostEstimate(flops=flops, bytes_accessed=bytes_accessed, transcendentals=0),
        **kw,
    )


def attend_kernel(start_ref, q_ref, *rest):
    blocks = rest[: REACH + 1]
    out_ref, bias_ref = rest[REACH + 1 :]
    row = lax.broadcasted_iota(jnp.int32, (ROWS, ROWS), 0)
    col = lax.broadcasted_iota(jnp.int32, (ROWS, ROWS), 1)
    lower = jnp.maximum(start_ref[...], row[:, :1] - (WINDOW - 1))
    for k in range(REACH + 1):
        place = col - k * ROWS
        allowed = place >= lower
        if k == 0:
            allowed = allowed & (place <= row)
        bias_ref[k] = jnp.where(allowed, 0.0, NEG)
    scale = HEAD_DIM ** (-0.5) * LOG2E

    def pair(index, carry):
        both = q_ref[:, pl.ds(pl.multiple_of(index * 256, 256), 256)]
        q = jnp.concatenate([both[:, :128], both[:, 128:]], axis=0)
        at = pl.multiple_of((index // 2) * 128, 128)
        scores = []
        highest = None
        for k in range(REACH + 1):
            s = lax.dot_general(
                q,
                blocks[k][:, pl.ds(at, 128)],
                (((1,), (1,)), ((), ())),
                preferred_element_type=F32,
            )
            bias = bias_ref[k]
            s = s * scale + jnp.concatenate([bias, bias], axis=0)
            scores.append(s)
            highest = s if highest is None else jnp.maximum(highest, s)
        top = jnp.max(highest, axis=-1, keepdims=True)
        total = None
        blended = None
        for k in range(REACH + 1):
            p = jnp.exp2(scores[k] - top)
            total = p if total is None else total + p
            part = jnp.dot(
                p.astype(BF16),
                blocks[k][:, pl.ds(pl.multiple_of(at + 256, 128), 128)],
                preferred_element_type=F32,
            )
            blended = part if blended is None else blended + part
        blended = (blended / jnp.sum(total, axis=-1, keepdims=True)).astype(BF16)
        out_ref[:, pl.ds(pl.multiple_of(index * 256, 256), 256)] = jnp.concatenate(
            [blended[:ROWS], blended[ROWS:]], axis=1
        )
        return carry

    lax.fori_loop(0, 4, pair, 0)


def attend(start, queries, blocks):
    call = vmem_call(
        attend_kernel,
        jax.ShapeDtypeStruct((ROWS, 1024), BF16),
        2 + REACH + 1,
        scratch=[pltpu.VMEM((REACH + 1, ROWS, ROWS), F32)],
        flops=5_000_000_000,
        bytes_accessed=4 << 20,
    )
    return call(start, queries, *blocks)


def conv_part(raw, rim, taps, start, row):
    wide = raw.astype(F32)
    early = rim.astype(F32)
    total = wide * taps[CONV - 1 : CONV].astype(F32)
    for back in range(1, CONV):
        moved = pltpu.roll(wide, back, 0)
        head = pltpu.roll(early, back, 0)
        moved = jnp.concatenate([jnp.where(row[:8] < back, head, moved[:8]), moved[8:]], axis=0)
        keep = row - back >= start
        total = total + jnp.where(keep, moved * taps[CONV - 1 - back : CONV - back].astype(F32), 0.0)
    return total * jax.nn.sigmoid(total)


def prepare_kernel(
    start_ref, raw_ref, state_ref, rim_ref, step_raw_ref, bias_ref, decay_ref, taps_ref, state_taps_ref,
    spread_ref, inner_ref, in_ref, out_ref, running_ref, step_ref, piece_ref,
):
    start = start_ref[...]
    row = lax.broadcasted_iota(jnp.int32, (ROWS, 1), 0)
    state = conv_part(state_ref[...], rim_ref[:, 2048:], state_taps_ref[...], start, row).astype(BF16)
    read_in = state[:, :STATE]
    in_ref[...] = read_in
    out_ref[...] = state[:, STATE:]
    step = jax.nn.softplus(step_raw_ref[...] + bias_ref[...])
    step_ref[...] = step
    running = -jnp.exp(decay_ref[...]) * step
    reach = 1
    while reach < ROWS:
        running = running + jnp.where(row >= reach, pltpu.roll(running, reach, 0), 0.0)
        reach *= 2
    running_ref[...] = running
    last = running[ROWS - 1 :]
    last_start = start[ROWS - 1 :]
    tail = jnp.where(row >= last_start, jnp.exp(last - running), 0.0) * step
    final = jnp.where(last_start < 0, jnp.exp(last), 0.0)
    spread = spread_ref[...]
    tail_wide = exact_spread(tail, spread)
    final_wide = exact_spread(jnp.broadcast_to(final, (16, final.shape[1])), spread)
    high = final_wide.astype(BF16)
    low = (final_wide - high.astype(F32)).astype(BF16)
    line = lax.broadcasted_iota(jnp.int32, (16, 1), 0)
    decays = jnp.where(line == 0, high.astype(F32), low.astype(F32)).astype(BF16)
    for j in range(CONTEXT):
        cols = slice(j * PIECE, (j + 1) * PIECE)
        inner = conv_part(raw_ref[:, cols], rim_ref[:, cols], taps_ref[:, cols], start, row).astype(BF16)
        inner_ref[:, cols] = inner
        weighted = (tail_wide[:, cols] * inner.astype(F32)).astype(BF16)
        piece = lax.dot_general(
            read_in, weighted, (((0,), (0,)), ((), ())), preferred_element_type=F32
        )
        piece_ref[j] = jnp.concatenate([piece.astype(BF16), decays[:, cols]], axis=0)


def exact_spread(values, spread):
    high = values.astype(BF16)
    rest = values - high.astype(F32)
    mid = rest.astype(BF16)
    low = (rest - mid.astype(F32)).astype(BF16)
    return (
        jnp.dot(high, spread, preferred_element_type=F32)
        + jnp.dot(mid, spread, preferred_element_type=F32)
        + jnp.dot(low, spread, preferred_element_type=F32)
    )


def within_kernel(
    start_ref, inner_ref, in_ref, out_ref, running_ref, step_ref, running_t_ref, step_t_ref, skip_ref, within_ref
):
    row = lax.broadcasted_iota(jnp.int32, (ROWS, ROWS), 0)
    col = lax.broadcasted_iota(jnp.int32, (ROWS, ROWS), 1)
    same = (col >= start_ref[...]) & (col <= row)
    pairwise = lax.dot_general(
        out_ref[...], in_ref[...], (((1,), (1,)), ((), ())), preferred_element_type=F32
    )
    pairwise = jnp.where(same, pairwise, 0.0)
    for j in range(CONTEXT):
        cols = slice(j * PIECE, (j + 1) * PIECE)
        inner = inner_ref[:, cols]
        parts = []
        for half in range(2):
            h = 2 * j + half
            gap = running_ref[:, h : h + 1] - running_t_ref[h : h + 1, :]
            decay = jnp.exp(jnp.minimum(gap, 0.0))
            mixing = (decay * pairwise * step_t_ref[h : h + 1, :]).astype(BF16)
            parts.append(jnp.dot(mixing, inner, preferred_element_type=F32))
        lane = lax.broadcasted_iota(jnp.int32, (ROWS, PIECE), 1)
        both = jnp.where(lane < 64, parts[0], parts[1])
        within_ref[:, cols] = both + skip_ref[:, cols] * inner.astype(F32)


def scan_kernel(piece_ref, out_ref):
    carried = jnp.zeros((STATE, PIECE), F32)
    for k in range(CONTEXT):
        out_ref[k] = carried.astype(BF16)
        decay = piece_ref[k, STATE : STATE + 1, :].astype(F32) + piece_ref[k, STATE + 1 : STATE + 2, :].astype(F32)
        carried = decay * carried + piece_ref[k, :STATE, :].astype(F32)


def finish_kernel(start_ref, within_ref, out_ref, running_ref, spread_ref, carried_ref, gate_ref, gated_ref, square_ref):
    entry = jnp.where(start_ref[...] < 0, jnp.exp(running_ref[...]), 0.0)
    entry_wide = exact_spread(entry, spread_ref[...])
    read_out = out_ref[...]
    squares = jnp.zeros((ROWS, PIECE), F32)
    for j in range(CONTEXT):
        cols = slice(j * PIECE, (j + 1) * PIECE)
        carried = jnp.dot(read_out, carried_ref[j], preferred_element_type=F32)
        ssm = within_ref[:, cols] + carried * entry_wide[:, cols]
        gate = gate_ref[:, cols].astype(F32)
        gated = ssm * (gate * jax.nn.sigmoid(gate))
        gated_ref[:, cols] = gated
        squares = squares + gated * gated
    square_ref[...] = jnp.sum(squares, axis=-1, keepdims=True)


def per_device(
    queries,
    key_states,
    value_states,
    segment_ids,
    hidden,
    attn_out_weight,
    norm_gain,
    gate_weight,
    inner_weight,
    state_proj_weight,
    step_weight,
    conv_inner,
    conv_state,
    step_bias,
    decay_log,
    skip_gain,
    out_gain,
):
    shape = jax.ShapeDtypeStruct
    anchor = lax.axis_index("context") * ROWS
    own = jnp.concatenate([key_states, value_states], axis=1)
    blocks = [own] + [shifted(own, k) for k in range(1, REACH + 1)]
    other_weight = swapped(attn_out_weight)
    query_seg = lax.dynamic_slice_in_dim(segment_ids, anchor, ROWS, 0)
    start = jnp.zeros((ROWS,), jnp.int32)
    for value in range(3):
        count = jnp.sum((segment_ids == value).astype(jnp.int32))
        start = start + jnp.where(query_seg > value, count, 0)
    start = (start - anchor)[:, None]

    attended = attend(start, queries, blocks)
    other = swapped(attended)
    mine = jnp.dot(attended, attn_out_weight, preferred_element_type=F32)
    theirs = jnp.dot(other, other_weight, preferred_element_type=F32)
    residual = (hidden.astype(F32) + (mine + theirs)).astype(BF16)
    wide = residual.astype(F32)
    normed = (
        wide
        * lax.rsqrt(jnp.mean(wide * wide, axis=-1, keepdims=True) + EPSILON)
        * norm_gain.astype(F32)[None, :]
    ).astype(BF16)
    inner_raw = jnp.dot(normed, inner_weight, preferred_element_type=F32).astype(BF16)
    state_raw = jnp.dot(normed, state_proj_weight, preferred_element_type=F32).astype(BF16)
    step_raw = jnp.dot(normed, step_weight, preferred_element_type=F32)
    rim = shifted(jnp.concatenate([inner_raw[ROWS - 8 :], state_raw[ROWS - 8 :]], axis=1), 1)
    gate = jnp.dot(normed, gate_weight, preferred_element_type=F32).astype(BF16)
    heads = step_weight.shape[1]
    spread = (jnp.arange(heads)[:, None] == jnp.arange(2048)[None, :] // 64).astype(BF16)
    inner, read_in, read_out, running, step, pieces = vmem_call(
        prepare_kernel,
        (
            shape((ROWS, 2048), BF16),
            shape((ROWS, STATE), BF16),
            shape((ROWS, STATE), BF16),
            shape((ROWS, heads), F32),
            shape((ROWS, heads), F32),
            shape((CONTEXT, PIECE_ROWS, PIECE), BF16),
        ),
        10,
        flops=1_000_000_000,
        bytes_accessed=3 << 20,
    )(
        start, inner_raw, state_raw, rim, step_raw, step_bias[None, :], decay_log[None, :],
        conv_inner, conv_state, spread,
    )
    gathered = lax.all_to_all(pieces, "context", 0, 0, tiled=True)
    skip = jnp.repeat(skip_gain, 64)[None, :]
    within = vmem_call(
        within_kernel, shape((ROWS, 2048), F32), 9, flops=3_000_000_000, bytes_accessed=4 << 20
    )(start, inner, read_in, read_out, running, step, running.T, step.T, skip)
    carried = vmem_call(
        scan_kernel, shape((CONTEXT, STATE, PIECE), BF16), 1, flops=1_000_000, bytes_accessed=1 << 20
    )(gathered)
    carried = lax.all_to_all(carried, "context", 0, 0, tiled=True)
    gated, squares = vmem_call(
        finish_kernel,
        (shape((ROWS, 2048), F32), shape((ROWS, 1), F32)),
        7,
        flops=1_000_000_000,
        bytes_accessed=6 << 20,
    )(start, within, read_out, running, spread, carried, gate)
    squares = lax.psum(squares[:, 0], "tensor")
    mixed = (
        gated * lax.rsqrt(squares / D_INNER + EPSILON)[:, None] * out_gain.astype(F32)[None, :]
    ).astype(BF16)
    return (residual, mixed)


def solution(mesh):
    in_specs = (
        P(("seq", "context"), "tensor"),
        P(("seq", "context"), "tensor"),
        P(("seq", "context"), "tensor"),
        P("seq"),
        P(("seq", "context"), None),
        P("tensor", None),
        P(),
        P(None, "tensor"),
        P(None, "tensor"),
        P(),
        P(None, "tensor"),
        P(None, "tensor"),
        P(),
        P("tensor"),
        P("tensor"),
        P("tensor"),
        P("tensor"),
    )
    out_specs = (P(("seq", "context"), None), P(("seq", "context"), "tensor"))
    return jax.shard_map(
        per_device, mesh=mesh, in_specs=in_specs, out_specs=out_specs, check_vma=False
    )
```

```python
import functools
import jax
import jax.numpy as jnp
from jax import lax
from jax.experimental import pallas as pl
from jax.experimental.pallas import tpu as pltpu
from jax.sharding import PartitionSpec as P

ATT_HEADS = 16
KV_HEADS = 4
HEAD_DIM = 128
STATE = 128
CONV = 4
WINDOW = 2048
D_INNER = 4096
ROWS = 256
REACH = 8
CONTEXT = 16
PIECE = 128
PIECE_ROWS = STATE + 16
EPSILON = 1e-05
NEG = -1e30
LOG2E = 1.4426950408889634


F32 = jnp.float32
BF16 = jnp.bfloat16


def moved(x, pairs):
    return lax.ppermute(x, "context", pairs)


def swapped(x):
    return lax.ppermute(x, "tensor", [(0, 1), (1, 0)])


def call(kernel, outs, ins, scratch=(), limit=16, flops=0, bytes_accessed=0):
    space = {"v": pltpu.VMEM, "s": pltpu.SMEM, "h": pltpu.HBM, "a": pl.ANY}
    single = len(outs) == 1
    shapes = tuple(
        pltpu.HBM(o[1], o[2]) if o[0] == "h" else jax.ShapeDtypeStruct(o[1], o[2]) for o in outs
    )
    specs = tuple(pl.BlockSpec(memory_space=space[o[0]]) for o in outs)
    run = pl.pallas_call(
        kernel,
        out_shape=shapes[0] if single else shapes,
        in_specs=[pl.BlockSpec(memory_space=space[k]) for k in ins],
        out_specs=specs[0] if single else specs,
        scratch_shapes=list(scratch),
        compiler_params=pltpu.CompilerParams(vmem_limit_bytes=limit << 20),
        cost_estimate=pl.CostEstimate(flops=flops, bytes_accessed=bytes_accessed, transcendentals=0),
    )

    def placed(*operands):
        return run(
            *(pltpu.with_memory_space_constraint(x, pltpu.HBM) if k == "h" else x for x, k in zip(operands, ins))
        )

    return placed


def fetch(source, target, semaphore):
    copy = pltpu.make_async_copy(source, target, semaphore)
    copy.start()
    return copy


def columns(n):
    return pl.ds(pl.multiple_of(n * 512, 512), 512)


def first_token(info_ref, row):
    start = info_ref[3]
    for v in range(3):
        start = jnp.maximum(start, jnp.where(info_ref[v] <= row, info_ref[v], info_ref[3]))
    return start


def pack_kernel(key_ref, value_ref, seg_ref, own_ref, info_ref, seg_v, sem):
    copies = [
        fetch(seg_ref, seg_v, sem.at[2]),
        fetch(key_ref, own_ref.at[:, :256], sem.at[0]),
        fetch(value_ref, own_ref.at[:, 256:], sem.at[1]),
    ]
    copies[0].wait()
    place = lax.axis_index("context")
    anchor = place * ROWS
    for v in range(3):
        below = jnp.where(seg_v[...] <= v, 1.0, 0.0)
        info_ref[v] = jnp.sum(below).astype(jnp.int32) - anchor
    info_ref[3] = -anchor
    info_ref[4] = lax.rem(place, 4)
    copies[1].wait()
    copies[2].wait()


def block_bias(place, lower):
    return jnp.where(place >= lower, 0.0, NEG)


def attend_pairs(q_ref, block_of, n_blocks, bias_ref, carry_in, finish):
    scale = HEAD_DIM ** (-0.5) * LOG2E

    def pair(index, carry):
        both = q_ref[:, pl.ds(pl.multiple_of(index * 256, 256), 256)]
        q = jnp.concatenate([both[:, :128], both[:, 128:]], axis=0)
        at = pl.multiple_of((index // 2) * 128, 128)
        scores = []
        highest = None
        for k in range(n_blocks):
            s = lax.dot_general(
                q, block_of(k, at), (((1,), (1,)), ((), ())), preferred_element_type=F32
            )
            bias = bias_ref[k]
            s = s * scale + jnp.concatenate([bias, bias], axis=0)
            scores.append(s)
            highest = s if highest is None else jnp.maximum(highest, s)
        top = jnp.max(highest, axis=-1, keepdims=True)
        before = None
        if carry_in is not None:
            before = carry_in[0][index][:, :1]
            top = jnp.maximum(top, before)
        total = None
        blended = None
        for k in range(n_blocks):
            p = jnp.exp2(scores[k] - top)
            total = p if total is None else total + p
            part = jnp.dot(
                p.astype(BF16),
                block_of(k, pl.multiple_of(at + 256, 128)),
                preferred_element_type=F32,
            )
            blended = part if blended is None else blended + part
        total = jnp.sum(total, axis=-1, keepdims=True)
        if carry_in is not None:
            alpha = jnp.exp2(before - top)
            total = total + alpha * carry_in[1][index][:, :1]
            blended = blended + alpha * carry_in[2][index]
        finish(index, top, total, blended)
        return carry

    lax.fori_loop(0, 4, pair, 0)


def attend_first_kernel(info_ref, q_hbm, own_ref, y1_hbm, y2_hbm, top_ref, total_ref, sum_ref, bias_ref, q_ref, y_ref, sem):
    copies = [
        fetch(q_hbm, q_ref, sem.at[0]),
        fetch(y1_hbm, y_ref.at[0], sem.at[1]),
        fetch(y2_hbm, y_ref.at[1], sem.at[2]),
    ]
    row = lax.broadcasted_iota(jnp.int32, (ROWS, ROWS), 0)
    col = lax.broadcasted_iota(jnp.int32, (ROWS, ROWS), 1)
    lower = jnp.maximum(first_token(info_ref, row), row - (WINDOW - 1))
    bias_ref[0] = jnp.where((col >= lower) & (col <= row), 0.0, NEG)
    bias_ref[1] = block_bias(col - 4 * ROWS, lower)
    bias_ref[2] = block_bias(col - 8 * ROWS, lower)
    for copy in copies:
        copy.wait()

    def block_of(k, at):
        return own_ref[:, pl.ds(at, 128)] if k == 0 else y_ref[k - 1, :, pl.ds(at, 128)]

    def finish(index, top, total, blended):
        top_ref[index] = jnp.broadcast_to(top, (2 * ROWS, 128))
        total_ref[index] = jnp.broadcast_to(total, (2 * ROWS, 128))
        sum_ref[index] = blended

    attend_pairs(q_ref, block_of, 3, bias_ref, None, finish)


def attend_rest_kernel(
    info_ref, q_hbm, p1, p2, p3, w1, w2, w3, r1, r2, r3, top_ref, total_ref, sum_ref, out_ref, bias_ref, block_ref, q_ref, sem
):
    z = info_ref[4]
    first = fetch(q_hbm, q_ref, sem.at[6])
    for s, (p, w) in enumerate(((p1, w1), (p2, w2), (p3, w3))):

        @pl.when(z >= s + 1)
        def _():
            pltpu.make_async_copy(p, block_ref.at[s], sem.at[s]).start()

        @pl.when(z < s + 1)
        def _():
            pltpu.make_async_copy(w, block_ref.at[s], sem.at[s]).start()

    for s, r in enumerate((r1, r2, r3)):
        pltpu.make_async_copy(r, block_ref.at[3 + s], sem.at[3 + s]).start()
    row = lax.broadcasted_iota(jnp.int32, (ROWS, ROWS), 0)
    col = lax.broadcasted_iota(jnp.int32, (ROWS, ROWS), 1)
    lower = jnp.maximum(first_token(info_ref, row), row - (WINDOW - 1))
    for s in range(3):
        near = z >= s + 1
        bias_ref[s] = block_bias(col - jnp.where(near, s + 1, s + 5) * ROWS, lower)
        bias_ref[3 + s] = block_bias(col - jnp.where(near, s + 5, s + 1) * ROWS, lower)
    first.wait()
    for s in range(6):
        pltpu.make_async_copy(r1, block_ref.at[s], sem.at[s]).wait()

    def finish(index, top, total, blended):
        blended = (blended / total).astype(BF16)
        out_ref[:, pl.ds(pl.multiple_of(index * 256, 256), 256)] = jnp.concatenate(
            [blended[:ROWS], blended[ROWS:]], axis=1
        )

    attend_pairs(
        q_ref, lambda k, at: block_ref[k, :, pl.ds(at, 128)], 6, bias_ref, (top_ref, total_ref, sum_ref), finish
    )


def attend(info, queries, own):
    near = range(4)
    y1 = moved(own, [(4 * y + x, 4 * y + 4 + x) for y in range(3) for x in near])
    y2 = moved(own, [(4 * y + x, 4 * y + 8 + x) for y in range(2) for x in near])
    p = [moved(own, [(4 * y + x, 4 * y + x + s) for y in near for x in near if x + s < 4]) for s in (1, 2, 3)]
    r = [moved(y1, [(4 * y + x, 4 * y + (x + s) % 4) for y in (1, 2, 3) for x in near]) for s in (1, 2, 3)]
    w = [moved(y2, [(4 * y + x, 4 * y + x + s - 4) for y in (2, 3) for x in near if x + s >= 4]) for s in (1, 2, 3)]
    part = ("v", (4, 2 * ROWS, 128), F32)
    carry = call(
        attend_first_kernel,
        [part] * 3,
        "shvaa",
        [
            pltpu.VMEM((3, ROWS, ROWS), F32),
            pltpu.VMEM((ROWS, 1024), BF16),
            pltpu.VMEM((2, ROWS, 512), BF16),
            pltpu.SemaphoreType.DMA((3,)),
        ],
        20,
        1_600_000_000,
        4 << 20,
    )(info, queries, own, y1, y2)
    return call(
        attend_rest_kernel,
        [("v", (ROWS, 1024), BF16)],
        "sh" + "a" * 9 + "vvv",
        [
            pltpu.VMEM((6, ROWS, ROWS), F32),
            pltpu.VMEM((6, ROWS, 512), BF16),
            pltpu.VMEM((ROWS, 1024), BF16),
            pltpu.SemaphoreType.DMA((7,)),
        ],
        24,
        3_400_000_000,
        4 << 20,
    )(info, queries, *p, *w, *r, *carry)


def own_part_kernel(x_ref, w_hbm, out_ref, w_ref, sem):
    for n in range(4):
        fetch(w_hbm.at[:, n * 512 : n * 512 + 512], w_ref.at[:, n * 512 : n * 512 + 512], sem.at[n])

    def tile(n, carry):
        cols = columns(n)
        pltpu.make_async_copy(w_hbm.at[:, cols], w_ref.at[:, cols], sem.at[n]).wait()
        out_ref[:, cols] = jnp.dot(x_ref[...], w_ref[:, cols], preferred_element_type=F32)
        return carry

    lax.fori_loop(0, 4, tile, 0)


def token_kernel(
    x_ref, w_hbm, mine_ref, hidden_hbm, gain_ref, inner_hbm, state_hbm, step_ref,
    residual_hbm, normed_ref, raw_ref, state_out_ref, step_out_ref, rim_ref,
    w_ref, hidden_ref, inner_ref, state_ref, theirs_ref, residual_ref, sem,
):
    for n in range(4):
        cols = slice(n * 512, n * 512 + 512)
        fetch(w_hbm.at[:, cols], w_ref.at[:, cols], sem.at[n])
        if n == 0:
            hidden = fetch(hidden_hbm, hidden_ref, sem.at[8])
    state = fetch(state_hbm, state_ref, sem.at[9])
    for n in range(4):
        cols = slice(n * 512, n * 512 + 512)
        fetch(inner_hbm.at[:, cols], inner_ref.at[:, cols], sem.at[4 + n])
    hidden.wait()

    def out_tile(n, squares):
        cols = columns(n)
        pltpu.make_async_copy(w_hbm.at[:, cols], w_ref.at[:, cols], sem.at[n]).wait()
        theirs_ref[...] = jnp.dot(x_ref[...], w_ref[:, cols], preferred_element_type=F32)
        total = hidden_ref[:, cols].astype(F32) + (mine_ref[:, cols] + theirs_ref[...])
        low = total.astype(BF16)
        residual_ref[:, cols] = low
        wide = low.astype(F32)
        wide = wide * wide
        return squares + (wide[:, :128] + wide[:, 128:256]) + (wide[:, 256:384] + wide[:, 384:])

    squares = lax.fori_loop(0, 4, out_tile, jnp.zeros((ROWS, 128), F32))
    residual = fetch(residual_ref, residual_hbm, sem.at[10])
    mean = jnp.sum(squares, axis=-1, keepdims=True) * (1.0 / 2048.0)
    scale = lax.rsqrt(mean + EPSILON)
    for n in range(4):
        cols = slice(n * 512, (n + 1) * 512)
        normed_ref[:, cols] = (
            residual_ref[:, cols].astype(F32) * scale * gain_ref[:, cols].astype(F32)
        ).astype(BF16)
    state.wait()
    narrow = jnp.dot(normed_ref[...], state_ref[...], preferred_element_type=F32).astype(BF16)
    state_out_ref[...] = narrow
    rim_ref[:, 2048:] = narrow[ROWS - 16 :]
    step_out_ref[...] = lax.dot_general(
        normed_ref[...], step_ref[...], (((1,), (1,)), ((), ())), preferred_element_type=F32
    )

    def in_tile(n, carry):
        cols = columns(n)
        pltpu.make_async_copy(inner_hbm.at[:, cols], inner_ref.at[:, cols], sem.at[4 + n]).wait()
        raw = jnp.dot(normed_ref[...], inner_ref[:, cols], preferred_element_type=F32).astype(BF16)
        raw_ref[:, cols] = raw
        rim_ref[:, cols] = raw[ROWS - 16 :]
        return carry

    lax.fori_loop(0, 4, in_tile, 0)
    residual.wait()


def gate_kernel(x_hbm, w_hbm, out_ref, x_ref, w_ref, sem):
    first = fetch(x_hbm, x_ref, sem.at[4])
    for n in range(4):
        fetch(w_hbm.at[:, n * 512 : n * 512 + 512], w_ref.at[:, n * 512 : n * 512 + 512], sem.at[n])
    first.wait()

    def tile(n, carry):
        cols = columns(n)
        pltpu.make_async_copy(w_hbm.at[:, cols], w_ref.at[:, cols], sem.at[n]).wait()
        out_ref[:, cols] = jnp.dot(x_ref[...], w_ref[:, cols], preferred_element_type=F32).astype(BF16)
        return carry

    lax.fori_loop(0, 4, tile, 0)


def scale_kernel(gated_ref, mine_ref, theirs_ref, gain_ref, out_ref):
    squares = jnp.broadcast_to(mine_ref[...] + theirs_ref[...], (128, ROWS))
    scale = lax.rsqrt(jnp.transpose(squares) * (1.0 / D_INNER) + EPSILON)
    for j in range(CONTEXT):
        cols = slice(j * PIECE, (j + 1) * PIECE)
        out_ref[:, cols] = (gated_ref[:, cols] * scale * gain_ref[:, cols].astype(F32)).astype(BF16)


def conv_part(raw, rim, taps, start, row):
    wide = raw.astype(F32)
    early = rim.astype(F32)[8:]
    total = wide * taps[CONV - 1 : CONV].astype(F32)
    for back in range(1, CONV):
        moved = pltpu.roll(wide, back, 0)
        head = pltpu.roll(early, back, 0)
        moved = jnp.concatenate([jnp.where(row[:8] < back, head, moved[:8]), moved[8:]], axis=0)
        keep = row - back >= start
        total = total + jnp.where(keep, moved * taps[CONV - 1 - back : CONV - back].astype(F32), 0.0)
    return total * jax.nn.sigmoid(total)


def spread_pair(values, j, lane):
    return jnp.where(lane < 64, values[:, 2 * j : 2 * j + 1], values[:, 2 * j + 1 : 2 * j + 2])


def prepare_kernel(
    info_ref, raw_ref, state_ref, rim_ref, step_raw_ref, bias_ref, decay_ref, taps_ref, state_taps_ref,
    inner_hbm, reads_hbm, running_hbm, rows_hbm, piece_ref,
    inner_ref, reads_ref, running_ref, rows_ref, sem,
):
    row = lax.broadcasted_iota(jnp.int32, (ROWS, 1), 0)
    wide_row = lax.broadcasted_iota(jnp.int32, (ROWS, PIECE), 0)
    lane = lax.broadcasted_iota(jnp.int32, (ROWS, PIECE), 1)
    start = first_token(info_ref, wide_row)
    state = [
        conv_part(
            state_ref[:, h * STATE : (h + 1) * STATE],
            rim_ref[:, 2048 + h * STATE : 2048 + (h + 1) * STATE],
            state_taps_ref[:, h * STATE : (h + 1) * STATE],
            start,
            wide_row,
        ).astype(BF16)
        for h in range(2)
    ]
    read_in = state[0]
    reads_ref[0] = read_in
    reads_ref[1] = state[1]
    step = jax.nn.softplus(step_raw_ref[...] + bias_ref[...])
    running = -jnp.exp(decay_ref[...]) * step
    reach = 1
    while reach < ROWS:
        running = running + jnp.where(row >= reach, pltpu.roll(running, reach, 0), 0.0)
        reach *= 2
    running_ref[...] = running
    rows_ref[0] = jnp.transpose(running)
    rows_ref[1] = jnp.transpose(step)
    copies = [
        fetch(reads_ref, reads_hbm, sem.at[0]),
        fetch(running_ref, running_hbm, sem.at[1]),
        fetch(rows_ref, rows_hbm, sem.at[2]),
    ]
    last = running[ROWS - 1 :]
    last_start = start[ROWS - 1 :, :1]
    tail = jnp.where(row >= last_start, jnp.exp(last - running), 0.0) * step
    final = jnp.where(last_start < 0, jnp.exp(last), 0.0)
    final = jnp.broadcast_to(final, (16, final.shape[1]))
    line = lax.broadcasted_iota(jnp.int32, (16, PIECE), 0)
    for j in range(CONTEXT):
        cols = slice(j * PIECE, (j + 1) * PIECE)
        inner = conv_part(raw_ref[:, cols], rim_ref[:, cols], taps_ref[:, cols], start, wide_row).astype(BF16)
        inner_ref[:, cols] = inner
        weighted = (spread_pair(tail, j, lane) * inner.astype(F32)).astype(BF16)
        piece = lax.dot_general(
            read_in, weighted, (((0,), (0,)), ((), ())), preferred_element_type=F32
        )
        decay = spread_pair(final, j, lane[:16])
        high = decay.astype(BF16).astype(F32)
        decays = jnp.where(line == 0, high, decay - high).astype(BF16)
        piece_ref[j] = jnp.concatenate([piece.astype(BF16), decays], axis=0)
        if j % 4 == 3:
            group = slice((j - 3) * PIECE, (j + 1) * PIECE)
            copies.append(fetch(inner_ref.at[:, group], inner_hbm.at[:, group], sem.at[3 + j // 4]))
    for copy in copies:
        copy.wait()


def within_kernel(
    info_ref, inner_hbm, reads_hbm, running_hbm, rows_hbm, skip_ref, within_ref,
    inner_ref, reads_ref, running_ref, rows_ref, sem,
):
    copies = [
        fetch(reads_hbm, reads_ref, sem.at[0]),
        fetch(running_hbm, running_ref, sem.at[1]),
        fetch(rows_hbm, rows_ref, sem.at[2]),
        fetch(inner_hbm, inner_ref, sem.at[3]),
    ]
    row = lax.broadcasted_iota(jnp.int32, (ROWS, ROWS), 0)
    col = lax.broadcasted_iota(jnp.int32, (ROWS, ROWS), 1)
    same = (col >= first_token(info_ref, row)) & (col <= row)
    lane = lax.broadcasted_iota(jnp.int32, (ROWS, PIECE), 1)
    for copy in copies:
        copy.wait()
    pairwise = lax.dot_general(
        reads_ref[1], reads_ref[0], (((1,), (1,)), ((), ())), preferred_element_type=F32
    )
    pairwise = jnp.where(same, pairwise, 0.0)
    for j in range(CONTEXT):
        cols = slice(j * PIECE, (j + 1) * PIECE)
        inner = inner_ref[:, cols]
        parts = []
        for half in range(2):
            h = 2 * j + half
            gap = running_ref[:, h : h + 1] - rows_ref[0, h : h + 1, :]
            decay = jnp.exp(jnp.minimum(gap, 0.0))
            mixing = (decay * pairwise * rows_ref[1, h : h + 1, :]).astype(BF16)
            parts.append(jnp.dot(mixing, inner, preferred_element_type=F32))
        both = jnp.where(lane < 64, parts[0], parts[1])
        within_ref[:, cols] = both + skip_ref[:, cols] * inner.astype(F32)


def scan_kernel(piece_ref, after_ref, out_ref):
    carried = jnp.zeros((STATE, PIECE), F32)
    for k in range(CONTEXT):
        out_ref[k] = carried.astype(BF16)
        decay = piece_ref[k, STATE : STATE + 1, :].astype(F32) + piece_ref[k, STATE + 1 : STATE + 2, :].astype(F32)
        carried = decay * carried + piece_ref[k, :STATE, :].astype(F32)


def finish_kernel(
    info_ref, within_ref, gate_ref, reads_hbm, running_hbm, carried_hbm, gated_ref, square_ref,
    read_ref, running_ref, carried_ref, sem,
):
    copies = [
        fetch(running_hbm, running_ref, sem.at[0]),
        fetch(reads_hbm.at[1], read_ref, sem.at[1]),
        fetch(carried_hbm, carried_ref, sem.at[2]),
    ]
    row = lax.broadcasted_iota(jnp.int32, (ROWS, 1), 0)
    lane = lax.broadcasted_iota(jnp.int32, (ROWS, PIECE), 1)
    open_row = first_token(info_ref, row) < 0
    for copy in copies:
        copy.wait()
    entry = jnp.where(open_row, jnp.exp(running_ref[...]), 0.0)
    read_out = read_ref[...]
    squares = jnp.zeros((ROWS, PIECE), F32)
    for j in range(CONTEXT):
        cols = slice(j * PIECE, (j + 1) * PIECE)
        carried = jnp.dot(read_out, carried_ref[j], preferred_element_type=F32)
        ssm = within_ref[:, cols] + carried * spread_pair(entry, j, lane)
        gate = gate_ref[:, cols].astype(F32)
        gated = ssm * (gate * jax.nn.sigmoid(gate))
        gated_ref[:, cols] = gated
        squares = squares + gated * gated
    square_ref[...] = jnp.sum(jnp.transpose(squares), axis=0, keepdims=True)


def per_device(
    queries,
    key_states,
    value_states,
    segment_ids,
    hidden,
    attn_out_weight,
    norm_gain,
    gate_weight,
    inner_weight,
    state_proj_weight,
    step_weight,
    conv_inner,
    conv_state,
    step_bias,
    decay_log,
    skip_gain,
    out_gain,
):
    heads = step_weight.shape[1]
    dma = pltpu.SemaphoreType.DMA
    own, info = call(
        pack_kernel,
        [("v", (ROWS, 512), BF16), ("s", (8,), jnp.int32)],
        "hhh",
        [pltpu.VMEM((32, 128), jnp.int32), dma((3,))],
        4,
    )(key_states, value_states, segment_ids.reshape(32, 128))
    other_weight = swapped(attn_out_weight)
    attended = attend(info, queries, own)
    other = swapped(attended)
    mine = call(
        own_part_kernel,
        [("v", (ROWS, 2048), F32)],
        "vh",
        [pltpu.VMEM((1024, 2048), BF16), dma((4,))],
        16,
        1_100_000_000,
        4 << 20,
    )(attended, attn_out_weight)
    residual, normed, inner_raw, state_raw, step_raw, rim = call(
        token_kernel,
        [
            ("h", (ROWS, 2048), BF16),
            ("v", (ROWS, 2048), BF16),
            ("v", (ROWS, 2048), BF16),
            ("v", (ROWS, 256), BF16),
            ("v", (ROWS, heads), F32),
            ("v", (16, 2304), BF16),
        ],
        "vavhvhhv",
        [
            pltpu.VMEM((1024, 2048), BF16),
            pltpu.VMEM((ROWS, 2048), BF16),
            pltpu.VMEM((2048, 2048), BF16),
            pltpu.VMEM((2048, 256), BF16),
            pltpu.VMEM((ROWS, 512), F32),
            pltpu.VMEM((ROWS, 2048), BF16),
            dma((11,)),
        ],
        32,
        3_600_000_000,
        14 << 20,
    )(other, other_weight, mine, hidden, norm_gain[None, :], inner_weight, state_proj_weight, step_weight.T)
    rim = moved(rim, [(i, i + 1) for i in range(CONTEXT - 1)])
    gate = call(
        gate_kernel,
        [("v", (ROWS, 2048), BF16)],
        "ah",
        [pltpu.VMEM((ROWS, 2048), BF16), pltpu.VMEM((2048, 2048), BF16), dma((5,))],
        20,
        2_200_000_000,
        9 << 20,
    )(normed, gate_weight)
    buffers = [
        pltpu.VMEM((ROWS, 2048), BF16),
        pltpu.VMEM((2, ROWS, STATE), BF16),
        pltpu.VMEM((ROWS, heads), F32),
        pltpu.VMEM((2, heads, ROWS), F32),
    ]
    inner, reads, running, rows, pieces = call(
        prepare_kernel,
        [
            ("h", (ROWS, 2048), BF16),
            ("h", (2, ROWS, STATE), BF16),
            ("h", (ROWS, heads), F32),
            ("h", (2, heads, ROWS), F32),
            ("v", (CONTEXT, PIECE_ROWS, PIECE), BF16),
        ],
        "svvvvvvvv",
        buffers + [dma((7,))],
        16,
        1_000_000_000,
        3 << 20,
    )(info, inner_raw, state_raw, rim, step_raw, step_bias[None, :], decay_log[None, :], conv_inner, conv_state)
    gathered = lax.all_to_all(pieces, "context", 0, 0, tiled=True)
    skip = jnp.repeat(skip_gain, 64)[None, :]
    within = call(
        within_kernel,
        [("v", (ROWS, 2048), F32)],
        "shhhhv",
        buffers + [dma((4,))],
        16,
        3_000_000_000,
        4 << 20,
    )(info, inner, reads, running, rows, skip)
    carried = call(
        scan_kernel, [("v", (CONTEXT, STATE, PIECE), BF16)], "va", (), 8, 1_000_000, 1 << 20
    )(gathered, within)
    carried = lax.all_to_all(carried, "context", 0, 0, tiled=True)
    gated, squares = call(
        finish_kernel,
        [("v", (ROWS, 2048), F32), ("v", (1, ROWS), F32)],
        "svvhhh",
        [
            pltpu.VMEM((ROWS, STATE), BF16),
            pltpu.VMEM((ROWS, heads), F32),
            pltpu.VMEM((CONTEXT, STATE, PIECE), BF16),
            dma((3,)),
        ],
        16,
        1_000_000_000,
        6 << 20,
    )(info, within, gate, reads, running, carried)
    mixed = call(
        scale_kernel, [("v", (ROWS, 2048), BF16)], "vvvv", (), 8, 2_000_000, 3 << 20
    )(gated, squares, swapped(squares), out_gain[None, :])
    return (residual, mixed)


def solution(mesh):
    in_specs = (
        P(("seq", "context"), "tensor"),
        P(("seq", "context"), "tensor"),
        P(("seq", "context"), "tensor"),
        P("seq"),
        P(("seq", "context"), None),
        P("tensor", None),
        P(),
        P(None, "tensor"),
        P(None, "tensor"),
        P(),
        P(None, "tensor"),
        P(None, "tensor"),
        P(),
        P("tensor"),
        P("tensor"),
        P("tensor"),
        P("tensor"),
    )
    out_specs = (P(("seq", "context"), None), P(("seq", "context"), "tensor"))
    return jax.shard_map(
        per_device, mesh=mesh, in_specs=in_specs, out_specs=out_specs, check_vma=False
    )
```

```python
import functools
import jax
import jax.numpy as jnp
from jax import lax
from jax.experimental import pallas as pl
from jax.experimental.pallas import tpu as pltpu
from jax.sharding import PartitionSpec as P

ATT_HEADS = 16
KV_HEADS = 4
HEAD_DIM = 128
STATE = 128
CONV = 4
WINDOW = 2048
D_INNER = 4096
ROWS = 256
REACH = 8
CONTEXT = 16
PIECE = 128
PIECE_ROWS = STATE + 16
EPSILON = 1e-05
NEG = -1e30
LOG2E = 1.4426950408889634


F32 = jnp.float32
BF16 = jnp.bfloat16


def moved(x, pairs):
    return lax.ppermute(x, "context", pairs)


def swapped(x):
    return lax.ppermute(x, "tensor", [(0, 1), (1, 0)])


def call(kernel, outs, ins, scratch=(), limit=16, flops=0, bytes_accessed=0, flags=None):
    space = {"v": pltpu.VMEM, "s": pltpu.SMEM, "h": pltpu.HBM, "a": pl.ANY}
    single = len(outs) == 1
    shapes = tuple(
        pltpu.HBM(o[1], o[2]) if o[0] == "h" else jax.ShapeDtypeStruct(o[1], o[2]) for o in outs
    )
    specs = tuple(pl.BlockSpec(memory_space=space[o[0]]) for o in outs)
    run = pl.pallas_call(
        kernel,
        out_shape=shapes[0] if single else shapes,
        in_specs=[pl.BlockSpec(memory_space=space[k]) for k in ins],
        out_specs=specs[0] if single else specs,
        scratch_shapes=list(scratch),
        compiler_params=pltpu.CompilerParams(vmem_limit_bytes=limit << 20, flags=flags),
        cost_estimate=pl.CostEstimate(flops=flops, bytes_accessed=bytes_accessed, transcendentals=0),
    )

    def placed(*operands):
        return run(
            *(pltpu.with_memory_space_constraint(x, pltpu.HBM) if k == "h" else x for x, k in zip(operands, ins))
        )

    return placed


def fetch(source, target, semaphore):
    copy = pltpu.make_async_copy(source, target, semaphore)
    copy.start()
    return copy


def columns(n):
    return pl.ds(pl.multiple_of(n * 512, 512), 512)


def first_token(info_ref, row):
    start = info_ref[3]
    for v in range(3):
        start = jnp.maximum(start, jnp.where(info_ref[v] <= row, info_ref[v], info_ref[3]))
    return start


def pack_kernel(key_ref, value_ref, seg_ref, own_ref, info_ref, seg_v, sem):
    copies = [
        fetch(seg_ref, seg_v, sem.at[2]),
        fetch(key_ref, own_ref.at[:, :256], sem.at[0]),
        fetch(value_ref, own_ref.at[:, 256:], sem.at[1]),
    ]
    copies[0].wait()
    place = lax.axis_index("context")
    anchor = place * ROWS
    for v in range(3):
        below = jnp.where(seg_v[...] <= v, 1.0, 0.0)
        info_ref[v] = jnp.sum(below).astype(jnp.int32) - anchor
    info_ref[3] = -anchor
    info_ref[4] = lax.rem(place, 4)
    copies[1].wait()
    copies[2].wait()


def block_bias(place, lower):
    return jnp.where(place >= lower, 0.0, NEG)


def attend_pairs(q_ref, block_ref, n, bias_ref, s_refs, p_refs, carry_in, finish):
    scale = HEAD_DIM ** (-0.5) * LOG2E
    wide = n * ROWS
    chunk = 32
    ones = jnp.ones((wide, 128), BF16)

    def group(g, carry):
        at = pl.multiple_of(g * 128, 128)
        keys = block_ref[:, :, pl.ds(at, 128)].reshape(wide, 128)
        for half in range(2):
            from_col = pl.multiple_of(g * 512 + half * 256, 256)
            both = q_ref[:, pl.ds(from_col, 256)]
            q = jnp.concatenate([both[:, :128], both[:, 128:]], axis=0)
            s_refs[half][...] = lax.dot_general(
                q, keys, (((1,), (1,)), ((), ())), preferred_element_type=F32
            )
        values = block_ref[:, :, pl.ds(pl.multiple_of(at + 256, 128), 128)].reshape(wide, 128)
        values = jnp.concatenate([values, ones], axis=1)
        for half in range(2):
            index = 2 * g + half
            for c in range(2 * ROWS // chunk):
                rows = slice(c * chunk, (c + 1) * chunk)
                from_row = (c * chunk) % ROWS
                s = s_refs[half][rows] * scale + bias_ref[from_row : from_row + chunk]
                top = jnp.max(s, axis=-1, keepdims=True)
                if carry_in is not None:
                    before = carry_in[3][index, rows]
                    top = jnp.maximum(top, before)
                    alpha = jnp.exp2(before - top)
                    carry_in[0][index, rows] = alpha
                    top = top[:, :1]
                p_refs[half][rows] = jnp.exp2(s - top).astype(BF16)
                if carry_in is None:
                    finish[0][index, rows] = jnp.broadcast_to(top, (chunk, 128))
            both = jnp.dot(p_refs[half][...], values, preferred_element_type=F32)
            blended, total = both[:, :128], both[:, 128:]
            if carry_in is None:
                finish[1][index] = total
                finish[2][index] = blended
            else:
                alpha = carry_in[0][index]
                total = total + alpha * carry_in[1][index]
                blended = ((blended + alpha * carry_in[2][index]) / total).astype(BF16)
                finish[:, pl.ds(pl.multiple_of(index * 256, 256), 256)] = jnp.concatenate(
                    [blended[:ROWS], blended[ROWS:]], axis=1
                )
        return carry

    lax.fori_loop(0, 2, group, 0)


def attend_scratch(n, extra=()):
    return [
        pltpu.VMEM((ROWS, n * ROWS), F32),
        pltpu.VMEM((n, ROWS, 512), BF16),
        pltpu.VMEM((ROWS, 1024), BF16),
        pltpu.VMEM((2 * ROWS, n * ROWS), F32),
        pltpu.VMEM((2 * ROWS, n * ROWS), F32),
        pltpu.VMEM((2 * ROWS, n * ROWS), BF16),
        pltpu.VMEM((2 * ROWS, n * ROWS), BF16),
        *extra,
        pltpu.SemaphoreType.DMA((n + 1,)),
    ]


def attend_first_kernel(
    info_ref, q_hbm, own_ref, y1_hbm, y2_hbm, p1, p2, p3, w1, w2, w3, top_ref, total_ref, sum_ref,
    bias_ref, block_ref, q_ref, s0, s1, e0, e1, sem,
):
    z = info_ref[4]
    copies = [fetch(q_hbm, q_ref, sem.at[6])]
    for k, source in enumerate((own_ref, y1_hbm, y2_hbm)):
        copies.append(fetch(source, block_ref.at[k], sem.at[k]))
    for s, (p, w) in enumerate(((p1, w1), (p2, w2), (p3, w3))):

        @pl.when(z >= s + 1)
        def _():
            pltpu.make_async_copy(p, block_ref.at[3 + s], sem.at[3 + s]).start()

        @pl.when(z < s + 1)
        def _():
            pltpu.make_async_copy(w, block_ref.at[3 + s], sem.at[3 + s]).start()

    row = lax.broadcasted_iota(jnp.int32, (ROWS, ROWS), 0)
    col = lax.broadcasted_iota(jnp.int32, (ROWS, ROWS), 1)
    lower = jnp.maximum(first_token(info_ref, row), row - (WINDOW - 1))
    bias_ref[:, :ROWS] = jnp.where((col >= lower) & (col <= row), 0.0, NEG)
    bias_ref[:, ROWS : 2 * ROWS] = block_bias(col - 4 * ROWS, lower)
    bias_ref[:, 2 * ROWS : 3 * ROWS] = block_bias(col - 8 * ROWS, lower)
    for s in range(3):
        bias_ref[:, (s + 3) * ROWS : (s + 4) * ROWS] = block_bias(
            col - jnp.where(z >= s + 1, s + 1, s + 5) * ROWS, lower
        )
    for copy in copies:
        copy.wait()
    for s in range(3):
        pltpu.make_async_copy(p1, block_ref.at[3 + s], sem.at[3 + s]).wait()
    attend_pairs(q_ref, block_ref, 6, bias_ref, (s0, s1), (e0, e1), None, (top_ref, total_ref, sum_ref))


def attend_rest_kernel(
    info_ref, q_hbm, r1, r2, r3, top_ref, total_ref, sum_ref, out_ref,
    bias_ref, block_ref, q_ref, s0, s1, e0, e1, alpha_ref, sem,
):
    z = info_ref[4]
    copies = [fetch(q_hbm, q_ref, sem.at[3])]
    for s, r in enumerate((r1, r2, r3)):
        copies.append(fetch(r, block_ref.at[s], sem.at[s]))
    row = lax.broadcasted_iota(jnp.int32, (ROWS, 1), 0)
    col = lax.broadcasted_iota(jnp.int32, (ROWS, ROWS), 1)
    lower = jnp.maximum(first_token(info_ref, row), row - (WINDOW - 1))
    for s in range(3):
        bias_ref[:, s * ROWS : (s + 1) * ROWS] = block_bias(
            col - jnp.where(z >= s + 1, s + 5, s + 1) * ROWS, lower
        )
    for copy in copies:
        copy.wait()
    attend_pairs(
        q_ref, block_ref, 3, bias_ref, (s0, s1), (e0, e1), (alpha_ref, total_ref, sum_ref, top_ref), out_ref
    )


def attend(info, queries, own):
    near = range(4)
    y1 = moved(own, [(4 * y + x, 4 * y + 4 + x) for y in range(3) for x in near])
    y2 = moved(own, [(4 * y + x, 4 * y + 8 + x) for y in range(2) for x in near])
    p = [moved(own, [(4 * y + x, 4 * y + x + s) for y in near for x in near if x + s < 4]) for s in (1, 2, 3)]
    r = [moved(y1, [(4 * y + x, 4 * y + (x + s) % 4) for y in (1, 2, 3) for x in near]) for s in (1, 2, 3)]
    w = [moved(y2, [(4 * y + x, 4 * y + x + s - 4) for y in (2, 3) for x in near if x + s >= 4]) for s in (1, 2, 3)]
    part = ("v", (4, 2 * ROWS, 128), F32)
    carry = call(
        attend_first_kernel, [part] * 3, "shaaa" + "a" * 6, attend_scratch(6), 32, 3_400_000_000, 4 << 20
    )(info, queries, own, y1, y2, *p, *w)
    return call(
        attend_rest_kernel,
        [("v", (ROWS, 1024), BF16)],
        "shaaavvv",
        attend_scratch(3, [pltpu.VMEM((4, 2 * ROWS, 128), F32)]),
        24,
        1_600_000_000,
        4 << 20,
    )(info, queries, *r, *carry)


def own_part_kernel(x_ref, w_hbm, out_ref, w_ref, sem):
    for n in range(4):
        fetch(w_hbm.at[:, n * 512 : n * 512 + 512], w_ref.at[:, n * 512 : n * 512 + 512], sem.at[n])

    def tile(n, carry):
        cols = columns(n)
        pltpu.make_async_copy(w_hbm.at[:, cols], w_ref.at[:, cols], sem.at[n]).wait()
        out_ref[:, cols] = jnp.dot(x_ref[...], w_ref[:, cols], preferred_element_type=F32)
        return carry

    lax.fori_loop(0, 4, tile, 0)


def token_kernel(
    x_ref, w_hbm, mine_ref, hidden_hbm, gain_ref, inner_hbm, state_hbm, step_ref,
    residual_hbm, normed_hbm, raw_ref, state_out_ref, step_out_ref, rim_ref,
    w_ref, hidden_ref, inner_ref, state_ref, theirs_ref, residual_ref, normed_ref, sem,
):
    for n in range(4):
        cols = slice(n * 512, n * 512 + 512)
        fetch(w_hbm.at[:, cols], w_ref.at[:, cols], sem.at[n])
        if n == 0:
            hidden = fetch(hidden_hbm, hidden_ref, sem.at[8])
    state = fetch(state_hbm, state_ref, sem.at[9])
    for n in range(4):
        cols = slice(n * 512, n * 512 + 512)
        fetch(inner_hbm.at[:, cols], inner_ref.at[:, cols], sem.at[4 + n])
    hidden.wait()

    squares = jnp.zeros((ROWS, 128), F32)
    for n in range(4):
        cols = slice(n * 512, n * 512 + 512)
        pltpu.make_async_copy(w_hbm.at[:, cols], w_ref.at[:, cols], sem.at[n]).wait()
        theirs_ref[:, cols] = jnp.dot(x_ref[...], w_ref[:, cols], preferred_element_type=F32)
        total = hidden_ref[:, cols].astype(F32) + (mine_ref[:, cols] + theirs_ref[:, cols])
        low = total.astype(BF16)
        residual_ref[:, cols] = low
        wide = low.astype(F32)
        wide = wide * wide
        squares = squares + (wide[:, :128] + wide[:, 128:256]) + (wide[:, 256:384] + wide[:, 384:])
    residual = fetch(residual_ref, residual_hbm, sem.at[10])
    mean = jnp.sum(squares, axis=-1, keepdims=True) * (1.0 / 2048.0)
    scale = lax.rsqrt(mean + EPSILON)
    for n in range(4):
        cols = slice(n * 512, (n + 1) * 512)
        normed_ref[:, cols] = (
            residual_ref[:, cols].astype(F32) * scale * gain_ref[:, cols].astype(F32)
        ).astype(BF16)
    normed = fetch(normed_ref, normed_hbm, sem.at[11])
    state.wait()
    narrow = jnp.dot(normed_ref[...], state_ref[...], preferred_element_type=F32).astype(BF16)
    state_out_ref[...] = narrow
    rim_ref[:, 2048:] = narrow[ROWS - 8 :]
    step_out_ref[...] = lax.dot_general(
        normed_ref[...], step_ref[...], (((1,), (1,)), ((), ())), preferred_element_type=F32
    )

    def in_tile(n, carry):
        cols = columns(n)
        pltpu.make_async_copy(inner_hbm.at[:, cols], inner_ref.at[:, cols], sem.at[4 + n]).wait()
        raw = jnp.dot(normed_ref[...], inner_ref[:, cols], preferred_element_type=F32).astype(BF16)
        raw_ref[:, cols] = raw
        rim_ref[:, cols] = raw[ROWS - 8 :]
        return carry

    lax.fori_loop(0, 4, in_tile, 0)
    residual.wait()
    normed.wait()


def gate_kernel(x_hbm, w_hbm, out_ref, x_ref, w_ref, sem):
    first = fetch(x_hbm, x_ref, sem.at[4])
    for n in range(4):
        fetch(w_hbm.at[:, n * 512 : n * 512 + 512], w_ref.at[:, n * 512 : n * 512 + 512], sem.at[n])
    first.wait()

    def tile(n, carry):
        cols = columns(n)
        pltpu.make_async_copy(w_hbm.at[:, cols], w_ref.at[:, cols], sem.at[n]).wait()
        out_ref[:, cols] = jnp.dot(x_ref[...], w_ref[:, cols], preferred_element_type=F32).astype(BF16)
        return carry

    lax.fori_loop(0, 4, tile, 0)


def scale_kernel(gated_ref, mine_ref, theirs_ref, gain_ref, out_ref):
    squares = jnp.broadcast_to(mine_ref[...] + theirs_ref[...], (128, ROWS))
    scale = lax.rsqrt(jnp.transpose(squares) * (1.0 / D_INNER) + EPSILON)
    for j in range(CONTEXT):
        cols = slice(j * PIECE, (j + 1) * PIECE)
        out_ref[:, cols] = (gated_ref[:, cols] * scale * gain_ref[:, cols].astype(F32)).astype(BF16)


def conv_part(raw, rim, taps, moves, start, row):
    early = rim.astype(F32)
    taps = taps.astype(F32)
    total = raw.astype(F32) * taps[CONV - 1 : CONV]
    edge = jnp.zeros_like(early)
    for back in range(1, CONV):
        tap = taps[CONV - 1 - back : CONV - back]
        total = total + jnp.dot(moves[back - 1], raw, preferred_element_type=F32) * tap
        keep = (row[:8] < back) & (row[:8] - back >= start[:8])
        edge = edge + jnp.where(keep, pltpu.roll(early, back, 0) * tap, 0.0)
    total = jnp.concatenate([total[:8] + edge, total[8:]], axis=0)
    return total * jax.nn.sigmoid(total)


def spread_pair(values, j, lane):
    return jnp.where(lane < 64, values[:, 2 * j : 2 * j + 1], values[:, 2 * j + 1 : 2 * j + 2])


def prepare_kernel(
    info_ref, raw_ref, state_ref, rim_ref, step_raw_ref, bias_ref, decay_ref, taps_ref, state_taps_ref,
    inner_hbm, reads_hbm, running_hbm, rows_hbm, piece_ref,
    inner_ref, reads_ref, running_ref, rows_ref, moves_ref, sem,
):
    row = lax.broadcasted_iota(jnp.int32, (ROWS, 1), 0)
    wide_row = lax.broadcasted_iota(jnp.int32, (ROWS, ROWS), 0)
    col = lax.broadcasted_iota(jnp.int32, (ROWS, ROWS), 1)
    lane = lax.broadcasted_iota(jnp.int32, (ROWS, PIECE), 1)
    start = first_token(info_ref, wide_row)
    for back in range(1, CONV):
        chosen = (col == wide_row - back) & (col >= start)
        moves_ref[back - 1] = jnp.where(chosen, 1.0, 0.0).astype(BF16)
    moves = [moves_ref[k] for k in range(CONV - 1)]
    state = conv_part(state_ref[...], rim_ref[:, 2048:], state_taps_ref[...], moves, start, wide_row).astype(BF16)
    read_in = state[:, :STATE]
    reads_ref[0] = read_in
    reads_ref[1] = state[:, STATE:]
    step = jax.nn.softplus(step_raw_ref[...] + bias_ref[...])
    running = -jnp.exp(decay_ref[...]) * step
    reach = 1
    while reach < ROWS:
        running = running + jnp.where(row >= reach, pltpu.roll(running, reach, 0), 0.0)
        reach *= 2
    running_ref[...] = running
    rows_ref[0] = jnp.transpose(running)
    rows_ref[1] = jnp.transpose(step)
    copies = [
        fetch(reads_ref, reads_hbm, sem.at[0]),
        fetch(running_ref, running_hbm, sem.at[1]),
        fetch(rows_ref, rows_hbm, sem.at[2]),
    ]
    last = running[ROWS - 1 :]
    last_start = start[ROWS - 1 :, :1]
    tail = jnp.where(row >= last_start, jnp.exp(last - running), 0.0) * step
    final = jnp.where(last_start < 0, jnp.exp(last), 0.0)
    final = jnp.broadcast_to(final, (16, final.shape[1]))
    line = lax.broadcasted_iota(jnp.int32, (16, PIECE), 0)
    for n in range(8):
        cols = slice(n * 256, (n + 1) * 256)
        inner_ref[:, cols] = conv_part(
            raw_ref[:, cols], rim_ref[:, cols], taps_ref[:, cols], moves, start, wide_row
        ).astype(BF16)
        if n % 2 == 1:
            group = slice((n - 1) * 256, (n + 1) * 256)
            copies.append(fetch(inner_ref.at[:, group], inner_hbm.at[:, group], sem.at[3 + n // 2]))
    for j in range(CONTEXT):
        cols = slice(j * PIECE, (j + 1) * PIECE)
        weighted = (spread_pair(tail, j, lane) * inner_ref[:, cols].astype(F32)).astype(BF16)
        piece = lax.dot_general(
            read_in, weighted, (((0,), (0,)), ((), ())), preferred_element_type=F32
        )
        decay = spread_pair(final, j, lane[:16])
        high = decay.astype(BF16).astype(F32)
        decays = jnp.where(line == 0, high, decay - high).astype(BF16)
        piece_ref[j] = jnp.concatenate([piece.astype(BF16), decays], axis=0)
    for copy in copies:
        copy.wait()


def within_kernel(
    info_ref, inner_hbm, reads_hbm, running_hbm, rows_hbm, skip_ref, within_ref,
    inner_ref, reads_ref, running_ref, rows_ref, sem,
):
    copies = [
        fetch(reads_hbm, reads_ref, sem.at[0]),
        fetch(running_hbm, running_ref, sem.at[1]),
        fetch(rows_hbm, rows_ref, sem.at[2]),
        fetch(inner_hbm, inner_ref, sem.at[3]),
    ]
    row = lax.broadcasted_iota(jnp.int32, (ROWS, ROWS), 0)
    col = lax.broadcasted_iota(jnp.int32, (ROWS, ROWS), 1)
    same = (col >= first_token(info_ref, row)) & (col <= row)
    lane = lax.broadcasted_iota(jnp.int32, (ROWS, PIECE), 1)
    for copy in copies:
        copy.wait()
    pairwise = lax.dot_general(
        reads_ref[1], reads_ref[0], (((1,), (1,)), ((), ())), preferred_element_type=F32
    )
    pairwise = jnp.where(same, pairwise, 0.0)
    for j in range(CONTEXT):
        cols = slice(j * PIECE, (j + 1) * PIECE)
        inner = inner_ref[:, cols]
        parts = []
        for half in range(2):
            h = 2 * j + half
            gap = running_ref[:, h : h + 1] - rows_ref[0, h : h + 1, :]
            decay = jnp.exp(jnp.minimum(gap, 0.0))
            mixing = (decay * pairwise * rows_ref[1, h : h + 1, :]).astype(BF16)
            parts.append(jnp.dot(mixing, inner, preferred_element_type=F32))
        both = jnp.where(lane < 64, parts[0], parts[1])
        within_ref[:, cols] = both + skip_ref[:, cols] * inner.astype(F32)


def scan_kernel(piece_ref, after_ref, out_ref):
    carried = jnp.zeros((STATE, PIECE), F32)
    for k in range(CONTEXT):
        out_ref[k] = carried.astype(BF16)
        decay = piece_ref[k, STATE : STATE + 1, :].astype(F32) + piece_ref[k, STATE + 1 : STATE + 2, :].astype(F32)
        carried = decay * carried + piece_ref[k, :STATE, :].astype(F32)


def finish_kernel(
    info_ref, within_ref, gate_ref, reads_hbm, running_hbm, carried_hbm, gated_ref, square_ref,
    read_ref, running_ref, carried_ref, sem,
):
    copies = [
        fetch(running_hbm, running_ref, sem.at[0]),
        fetch(reads_hbm.at[1], read_ref, sem.at[1]),
        fetch(carried_hbm, carried_ref, sem.at[2]),
    ]
    row = lax.broadcasted_iota(jnp.int32, (ROWS, 1), 0)
    lane = lax.broadcasted_iota(jnp.int32, (ROWS, PIECE), 1)
    open_row = first_token(info_ref, row) < 0
    for copy in copies:
        copy.wait()
    entry = jnp.where(open_row, jnp.exp(running_ref[...]), 0.0)
    read_out = read_ref[...]
    squares = jnp.zeros((ROWS, PIECE), F32)
    for j in range(CONTEXT):
        cols = slice(j * PIECE, (j + 1) * PIECE)
        carried = jnp.dot(read_out, carried_ref[j], preferred_element_type=F32)
        ssm = within_ref[:, cols] + carried * spread_pair(entry, j, lane)
        gate = gate_ref[:, cols].astype(F32)
        gated = ssm * (gate * jax.nn.sigmoid(gate))
        gated_ref[:, cols] = gated
        squares = squares + gated * gated
    square_ref[...] = jnp.sum(jnp.transpose(squares), axis=0, keepdims=True)


def per_device(
    queries,
    key_states,
    value_states,
    segment_ids,
    hidden,
    attn_out_weight,
    norm_gain,
    gate_weight,
    inner_weight,
    state_proj_weight,
    step_weight,
    conv_inner,
    conv_state,
    step_bias,
    decay_log,
    skip_gain,
    out_gain,
):
    heads = step_weight.shape[1]
    dma = pltpu.SemaphoreType.DMA
    own, info = call(
        pack_kernel,
        [("v", (ROWS, 512), BF16), ("s", (8,), jnp.int32)],
        "hhh",
        [pltpu.VMEM((32, 128), jnp.int32), dma((3,))],
        4,
    )(key_states, value_states, segment_ids.reshape(32, 128))
    other_weight = swapped(attn_out_weight)
    attended = attend(info, queries, own)
    other = swapped(attended)
    mine = call(
        own_part_kernel,
        [("v", (ROWS, 2048), F32)],
        "vh",
        [pltpu.VMEM((1024, 2048), BF16), dma((4,))],
        16,
        1_100_000_000,
        4 << 20,
    )(attended, attn_out_weight)
    residual, normed, inner_raw, state_raw, step_raw, rim = call(
        token_kernel,
        [
            ("h", (ROWS, 2048), BF16),
            ("h", (ROWS, 2048), BF16),
            ("v", (ROWS, 2048), BF16),
            ("v", (ROWS, 256), BF16),
            ("v", (ROWS, heads), F32),
            ("v", (8, 2304), BF16),
        ],
        "vavhvhhv",
        [
            pltpu.VMEM((1024, 2048), BF16),
            pltpu.VMEM((ROWS, 2048), BF16),
            pltpu.VMEM((2048, 2048), BF16),
            pltpu.VMEM((2048, 256), BF16),
            pltpu.VMEM((ROWS, 2048), F32),
            pltpu.VMEM((ROWS, 2048), BF16),
            pltpu.VMEM((ROWS, 2048), BF16),
            dma((12,)),
        ],
        32,
        3_600_000_000,
        14 << 20,
    )(other, other_weight, mine, hidden, norm_gain[None, :], inner_weight, state_proj_weight, step_weight.T)
    rim = moved(rim, [(i, i + 1) for i in range(CONTEXT - 1)])
    gate = call(
        gate_kernel,
        [("v", (ROWS, 2048), BF16)],
        "hh",
        [pltpu.VMEM((ROWS, 2048), BF16), pltpu.VMEM((2048, 2048), BF16), dma((5,))],
        20,
        2_200_000_000,
        9 << 20,
    )(normed, gate_weight)
    buffers = [
        pltpu.VMEM((ROWS, 2048), BF16),
        pltpu.VMEM((2, ROWS, STATE), BF16),
        pltpu.VMEM((ROWS, heads), F32),
        pltpu.VMEM((2, heads, ROWS), F32),
    ]
    inner, reads, running, rows, pieces = call(
        prepare_kernel,
        [
            ("h", (ROWS, 2048), BF16),
            ("h", (2, ROWS, STATE), BF16),
            ("h", (ROWS, heads), F32),
            ("h", (2, heads, ROWS), F32),
            ("v", (CONTEXT, PIECE_ROWS, PIECE), BF16),
        ],
        "svvvvvvvv",
        buffers + [pltpu.VMEM((CONV - 1, ROWS, ROWS), BF16), dma((7,))],
        16,
        1_000_000_000,
        3 << 20,
    )(info, inner_raw, state_raw, rim, step_raw, step_bias[None, :], decay_log[None, :], conv_inner, conv_state)
    gathered = lax.all_to_all(pieces, "context", 0, 0, tiled=True)
    skip = jnp.repeat(skip_gain, 64)[None, :]
    within = call(
        within_kernel,
        [("v", (ROWS, 2048), F32)],
        "shhhhv",
        buffers + [dma((4,))],
        16,
        3_000_000_000,
        4 << 20,
    )(info, inner, reads, running, rows, skip)
    carried = call(
        scan_kernel, [("v", (CONTEXT, STATE, PIECE), BF16)], "va", (), 8, 1_000_000, 1 << 20
    )(gathered, within)
    carried = lax.all_to_all(carried, "context", 0, 0, tiled=True)
    gated, squares = call(
        finish_kernel,
        [("v", (ROWS, 2048), F32), ("v", (1, ROWS), F32)],
        "svvhha",
        [
            pltpu.VMEM((ROWS, STATE), BF16),
            pltpu.VMEM((ROWS, heads), F32),
            pltpu.VMEM((CONTEXT, STATE, PIECE), BF16),
            dma((3,)),
        ],
        16,
        1_000_000_000,
        6 << 20,
    )(info, within, gate, reads, running, carried)
    mixed = call(
        scale_kernel, [("v", (ROWS, 2048), BF16)], "vvvv", (), 8, 2_000_000, 3 << 20
    )(gated, squares, swapped(squares), out_gain[None, :])
    return (residual, mixed)


def solution(mesh):
    in_specs = (
        P(("seq", "context"), "tensor"),
        P(("seq", "context"), "tensor"),
        P(("seq", "context"), "tensor"),
        P("seq"),
        P(("seq", "context"), None),
        P("tensor", None),
        P(),
        P(None, "tensor"),
        P(None, "tensor"),
        P(),
        P(None, "tensor"),
        P(None, "tensor"),
        P(),
        P("tensor"),
        P("tensor"),
        P("tensor"),
        P("tensor"),
    )
    out_specs = (P(("seq", "context"), None), P(("seq", "context"), "tensor"))
    return jax.shard_map(
        per_device, mesh=mesh, in_specs=in_specs, out_specs=out_specs, check_vma=False
    )
```

```python
import functools
import jax
import jax.numpy as jnp
from jax import lax
from jax.experimental import pallas as pl
from jax.experimental.pallas import tpu as pltpu
from jax.sharding import PartitionSpec as P

ATT_HEADS = 16
KV_HEADS = 4
HEAD_DIM = 128
STATE = 128
CONV = 4
WINDOW = 2048
D_INNER = 4096
ROWS = 256
REACH = 8
CONTEXT = 16
PIECE = 128
PIECE_ROWS = STATE + 16
HEAD = 16
EPSILON = 1e-05
NEG = -1e30
LOG2E = 1.4426950408889634


F32 = jnp.float32
BF16 = jnp.bfloat16


def moved(x, pairs):
    return lax.ppermute(x, "context", pairs)


def swapped(x):
    return lax.ppermute(x, "tensor", [(0, 1), (1, 0)])


def call(kernel, outs, ins, scratch=(), limit=16, flops=0, bytes_accessed=0, flags=None):
    space = {"v": pltpu.VMEM, "s": pltpu.SMEM, "h": pltpu.HBM, "a": pl.ANY}
    single = len(outs) == 1
    shapes = tuple(
        pltpu.HBM(o[1], o[2]) if o[0] == "h" else jax.ShapeDtypeStruct(o[1], o[2]) for o in outs
    )
    specs = tuple(pl.BlockSpec(memory_space=space[o[0]]) for o in outs)
    run = pl.pallas_call(
        kernel,
        out_shape=shapes[0] if single else shapes,
        in_specs=[pl.BlockSpec(memory_space=space[k]) for k in ins],
        out_specs=specs[0] if single else specs,
        scratch_shapes=list(scratch),
        compiler_params=pltpu.CompilerParams(vmem_limit_bytes=limit << 20, flags=flags),
        cost_estimate=pl.CostEstimate(flops=flops, bytes_accessed=bytes_accessed, transcendentals=0),
    )

    def placed(*operands):
        return run(
            *(pltpu.with_memory_space_constraint(x, pltpu.HBM) if k == "h" else x for x, k in zip(operands, ins))
        )

    return placed


def fetch(source, target, semaphore):
    copy = pltpu.make_async_copy(source, target, semaphore)
    copy.start()
    return copy


def columns(n):
    return pl.ds(pl.multiple_of(n * 512, 512), 512)


def first_token(info_ref, row):
    start = info_ref[3]
    for v in range(3):
        start = jnp.maximum(start, jnp.where(info_ref[v] <= row, info_ref[v], info_ref[3]))
    return start


def pack_kernel(key_ref, value_ref, seg_ref, own_ref, info_ref, seg_v, sem):
    copies = [
        fetch(seg_ref, seg_v, sem.at[2]),
        fetch(key_ref, own_ref.at[:, :256], sem.at[0]),
        fetch(value_ref, own_ref.at[:, 256:], sem.at[1]),
    ]
    copies[0].wait()
    place = lax.axis_index("context")
    anchor = place * ROWS
    for v in range(3):
        below = jnp.where(seg_v[...] <= v, 1.0, 0.0)
        info_ref[v] = jnp.sum(below).astype(jnp.int32) - anchor
    info_ref[3] = -anchor
    info_ref[4] = lax.rem(place, 4)
    copies[1].wait()
    copies[2].wait()


def block_bias(place, lower):
    return jnp.where(place >= lower, 0.0, NEG)


def attend_pairs(q_ref, block_ref, n, bias_ref, s_refs, p_refs, carry_in, finish):
    scale = HEAD_DIM ** (-0.5) * LOG2E
    wide = n * ROWS
    chunk = 32
    ones = jnp.ones((wide, 128), BF16)

    def group(g, carry):
        at = pl.multiple_of(g * 128, 128)
        keys = block_ref[:, :, pl.ds(at, 128)].reshape(wide, 128)
        for half in range(2):
            from_col = pl.multiple_of(g * 512 + half * 256, 256)
            both = q_ref[:, pl.ds(from_col, 256)]
            q = jnp.concatenate([both[:, :128], both[:, 128:]], axis=0)
            s_refs[half][...] = lax.dot_general(
                q, keys, (((1,), (1,)), ((), ())), preferred_element_type=F32
            )
        values = block_ref[:, :, pl.ds(pl.multiple_of(at + 256, 128), 128)].reshape(wide, 128)
        values = jnp.concatenate([values, ones], axis=1)
        for half in range(2):
            index = 2 * g + half
            for c in range(2 * ROWS // chunk):
                rows = slice(c * chunk, (c + 1) * chunk)
                from_row = (c * chunk) % ROWS
                s = s_refs[half][rows] * scale + bias_ref[from_row : from_row + chunk]
                top = jnp.max(s, axis=-1, keepdims=True)
                if carry_in is not None:
                    before = carry_in[3][index, rows]
                    top = jnp.maximum(top, before)
                    alpha = jnp.exp2(before - top)
                    carry_in[0][index, rows] = alpha
                    top = top[:, :1]
                p_refs[half][rows] = jnp.exp2(s - top).astype(BF16)
                if carry_in is None:
                    finish[0][index, rows] = jnp.broadcast_to(top, (chunk, 128))
            both = jnp.dot(p_refs[half][...], values, preferred_element_type=F32)
            blended, total = both[:, :128], both[:, 128:]
            if carry_in is None:
                finish[1][index] = total
                finish[2][index] = blended
            else:
                alpha = carry_in[0][index]
                total = total + alpha * carry_in[1][index]
                blended = ((blended + alpha * carry_in[2][index]) / total).astype(BF16)
                finish[:, pl.ds(pl.multiple_of(index * 256, 256), 256)] = jnp.concatenate(
                    [blended[:ROWS], blended[ROWS:]], axis=1
                )
        return carry

    lax.fori_loop(0, 2, group, 0)


def attend_scratch(n, extra=()):
    return [
        pltpu.VMEM((ROWS, n * ROWS), F32),
        pltpu.VMEM((n, ROWS, 512), BF16),
        pltpu.VMEM((ROWS, 1024), BF16),
        pltpu.VMEM((2 * ROWS, n * ROWS), F32),
        pltpu.VMEM((2 * ROWS, n * ROWS), F32),
        pltpu.VMEM((2 * ROWS, n * ROWS), BF16),
        pltpu.VMEM((2 * ROWS, n * ROWS), BF16),
        *extra,
        pltpu.SemaphoreType.DMA((n + 1,)),
    ]


def attend_first_kernel(
    info_ref, q_hbm, own_ref, y1_hbm, y2_hbm, p1, p2, p3, w1, w2, w3, weight_hbm, mine_hbm,
    top_ref, total_ref, sum_ref, weight_ref, mine_ref,
    bias_ref, block_ref, q_ref, s0, s1, e0, e1, weight_sem, sem,
):
    z = info_ref[4]
    copies = [fetch(q_hbm, q_ref, sem.at[6])]
    for k, source in enumerate((own_ref, y1_hbm, y2_hbm)):
        copies.append(fetch(source, block_ref.at[k], sem.at[k]))
    for s, (p, w) in enumerate(((p1, w1), (p2, w2), (p3, w3))):

        @pl.when(z >= s + 1)
        def _():
            pltpu.make_async_copy(p, block_ref.at[3 + s], sem.at[3 + s]).start()

        @pl.when(z < s + 1)
        def _():
            pltpu.make_async_copy(w, block_ref.at[3 + s], sem.at[3 + s]).start()

    row = lax.broadcasted_iota(jnp.int32, (ROWS, ROWS), 0)
    col = lax.broadcasted_iota(jnp.int32, (ROWS, ROWS), 1)
    lower = jnp.maximum(first_token(info_ref, row), row - (WINDOW - 1))
    bias_ref[:, :ROWS] = jnp.where((col >= lower) & (col <= row), 0.0, NEG)
    bias_ref[:, ROWS : 2 * ROWS] = block_bias(col - 4 * ROWS, lower)
    bias_ref[:, 2 * ROWS : 3 * ROWS] = block_bias(col - 8 * ROWS, lower)
    for s in range(3):
        bias_ref[:, (s + 3) * ROWS : (s + 4) * ROWS] = block_bias(
            col - jnp.where(z >= s + 1, s + 1, s + 5) * ROWS, lower
        )
    for copy in copies:
        copy.wait()
    for s in range(3):
        pltpu.make_async_copy(p1, block_ref.at[3 + s], sem.at[3 + s]).wait()
    mine = fetch(mine_hbm, mine_ref, weight_sem.at[1])
    weight = fetch(weight_hbm, weight_ref, weight_sem.at[0])
    attend_pairs(q_ref, block_ref, 6, bias_ref, (s0, s1), (e0, e1), None, (top_ref, total_ref, sum_ref))
    weight.wait()
    mine.wait()


def attend_rest_kernel(
    info_ref, q_hbm, r1, r2, r3, top_ref, total_ref, sum_ref, weight_hbm, out_ref, weight_ref,
    bias_ref, block_ref, q_ref, s0, s1, e0, e1, alpha_ref, weight_sem, sem,
):
    z = info_ref[4]
    copies = [fetch(q_hbm, q_ref, sem.at[3])]
    for s, r in enumerate((r1, r2, r3)):
        copies.append(fetch(r, block_ref.at[s], sem.at[s]))
    row = lax.broadcasted_iota(jnp.int32, (ROWS, 1), 0)
    col = lax.broadcasted_iota(jnp.int32, (ROWS, ROWS), 1)
    lower = jnp.maximum(first_token(info_ref, row), row - (WINDOW - 1))
    for s in range(3):
        bias_ref[:, s * ROWS : (s + 1) * ROWS] = block_bias(
            col - jnp.where(z >= s + 1, s + 5, s + 1) * ROWS, lower
        )
    for copy in copies:
        copy.wait()
    weight = fetch(weight_hbm, weight_ref, weight_sem)
    attend_pairs(
        q_ref, block_ref, 3, bias_ref, (s0, s1), (e0, e1), (alpha_ref, total_ref, sum_ref, top_ref), out_ref
    )
    weight.wait()


def attend(info, queries, own, inner_weight, own_weight, other_weight):
    near = range(4)
    y1 = moved(own, [(4 * y + x, 4 * y + 4 + x) for y in range(3) for x in near])
    y2 = moved(own, [(4 * y + x, 4 * y + 8 + x) for y in range(2) for x in near])
    p = [moved(own, [(4 * y + x, 4 * y + x + s) for y in near for x in near if x + s < 4]) for s in (1, 2, 3)]
    r = [moved(y1, [(4 * y + x, 4 * y + (x + s) % 4) for y in (1, 2, 3) for x in near]) for s in (1, 2, 3)]
    w = [moved(y2, [(4 * y + x, 4 * y + x + s - 4) for y in (2, 3) for x in near if x + s >= 4]) for s in (1, 2, 3)]
    part = ("v", (4, 2 * ROWS, 128), F32)
    one = pltpu.SemaphoreType.DMA
    *carry, inner_near, own_near = call(
        attend_first_kernel,
        [part] * 3 + [("v", (2048, 2048), BF16), ("v", (1024, 2048), BF16)],
        "shaaa" + "a" * 6 + "hh",
        attend_scratch(6, [pltpu.SemaphoreType.DMA((2,))]),
        32,
        3_400_000_000,
        4 << 20,
    )(info, queries, own, y1, y2, *p, *w, inner_weight, own_weight)
    attended, other_near = call(
        attend_rest_kernel,
        [("v", (ROWS, 1024), BF16), ("v", (1024, 2048), BF16)],
        "shaaavvva",
        attend_scratch(3, [pltpu.VMEM((4, 2 * ROWS, 128), F32), one]),
        24,
        1_600_000_000,
        4 << 20,
    )(info, queries, *r, *carry, other_weight)
    return attended, inner_near, own_near, other_near


def own_part_kernel(x_ref, w_ref, out_ref):
    for n in range(4):
        cols = slice(n * 512, n * 512 + 512)
        out_ref[:, cols] = jnp.dot(x_ref[...], w_ref[:, cols], preferred_element_type=F32)


def token_kernel(
    x_ref, w_ref, mine_ref, hidden_hbm, gain_ref, inner_ref, state_hbm, step_ref,
    residual_hbm, normed_hbm, raw_ref, state_out_ref, step_out_ref, rim_ref,
    hidden_ref, state_ref, theirs_ref, residual_ref, normed_ref, sem,
):
    hidden = fetch(hidden_hbm, hidden_ref, sem.at[0])
    state = fetch(state_hbm, state_ref, sem.at[1])
    theirs_ref[:, :512] = jnp.dot(x_ref[...], w_ref[:, :512], preferred_element_type=F32)
    hidden.wait()
    squares = jnp.zeros((ROWS, 128), F32)
    for n in range(4):
        cols = slice(n * 512, n * 512 + 512)
        if n > 0:
            theirs_ref[:, cols] = jnp.dot(x_ref[...], w_ref[:, cols], preferred_element_type=F32)
        total = hidden_ref[:, cols].astype(F32) + (mine_ref[:, cols] + theirs_ref[:, cols])
        low = total.astype(BF16)
        residual_ref[:, cols] = low
        wide = low.astype(F32)
        wide = wide * wide
        squares = squares + (wide[:, :128] + wide[:, 128:256]) + (wide[:, 256:384] + wide[:, 384:])
    residual = fetch(residual_ref, residual_hbm, sem.at[2])
    mean = jnp.sum(squares, axis=-1, keepdims=True) * (1.0 / 2048.0)
    scale = lax.rsqrt(mean + EPSILON)
    for n in range(4):
        cols = slice(n * 512, (n + 1) * 512)
        normed_ref[:, cols] = (
            residual_ref[:, cols].astype(F32) * scale * gain_ref[:, cols].astype(F32)
        ).astype(BF16)
    normed = fetch(normed_ref, normed_hbm, sem.at[3])
    state.wait()
    narrow = jnp.dot(normed_ref[...], state_ref[...], preferred_element_type=F32).astype(BF16)
    state_out_ref[...] = narrow
    rim_ref[:, 2048:] = narrow[ROWS - 8 :]
    step_out_ref[...] = lax.dot_general(
        normed_ref[...], step_ref[...], (((1,), (1,)), ((), ())), preferred_element_type=F32
    )

    def in_tile(n, carry):
        cols = columns(n)
        raw = jnp.dot(normed_ref[...], inner_ref[:, cols], preferred_element_type=F32).astype(BF16)
        raw_ref[:, cols] = raw
        rim_ref[:, cols] = raw[ROWS - 8 :]
        return carry

    lax.fori_loop(0, 4, in_tile, 0)
    residual.wait()
    normed.wait()


def gate_kernel(x_hbm, w_hbm, after_ref, out_ref, x_ref, w_ref, sem):
    first = fetch(x_hbm, x_ref, sem.at[4])
    for n in range(4):
        fetch(w_hbm.at[:, n * 512 : n * 512 + 512], w_ref.at[:, n * 512 : n * 512 + 512], sem.at[n])
    first.wait()

    def tile(n, carry):
        cols = columns(n)
        pltpu.make_async_copy(w_hbm.at[:, cols], w_ref.at[:, cols], sem.at[n]).wait()
        out_ref[:, cols] = jnp.dot(x_ref[...], w_ref[:, cols], preferred_element_type=F32).astype(BF16)
        return carry

    lax.fori_loop(0, 4, tile, 0)


def scale_kernel(gated_ref, mine_ref, theirs_ref, gain_ref, out_ref):
    squares = jnp.broadcast_to(mine_ref[...] + theirs_ref[...], (128, ROWS))
    scale = lax.rsqrt(jnp.transpose(squares) * (1.0 / D_INNER) + EPSILON)
    for j in range(CONTEXT):
        cols = slice(j * PIECE, (j + 1) * PIECE)
        out_ref[:, cols] = (gated_ref[:, cols] * scale * gain_ref[:, cols].astype(F32)).astype(BF16)


def conv_sum(raw, taps, moves):
    taps = taps.astype(F32)
    total = raw.astype(F32) * taps[CONV - 1 : CONV]
    for back in range(1, CONV):
        tap = taps[CONV - 1 - back : CONV - back]
        total = total + jnp.dot(moves[back - 1], raw, preferred_element_type=F32) * tap
    return total


def conv_edge(rim, taps, start, row):
    early = rim.astype(F32)
    taps = taps.astype(F32)
    edge = jnp.zeros_like(early)
    for back in range(1, CONV):
        tap = taps[CONV - 1 - back : CONV - back]
        keep = (row < back) & (row - back >= start)
        edge = edge + jnp.where(keep, pltpu.roll(early, back, 0) * tap, 0.0)
    return edge


def silu(x):
    return x * jax.nn.sigmoid(x)


def spread_pair(values, j, lane):
    return jnp.where(lane < 64, values[:, 2 * j : 2 * j + 1], values[:, 2 * j + 1 : 2 * j + 2])


def prepare_kernel(
    info_ref, raw_ref, state_ref, step_raw_ref, bias_ref, decay_ref, taps_ref, state_taps_ref,
    inner_hbm, reads_hbm, running_hbm, rows_hbm, piece_ref, decays_ref, head_ref, tail_ref,
    inner_ref, reads_ref, running_ref, rows_ref, moves_ref, sem,
):
    row = lax.broadcasted_iota(jnp.int32, (ROWS, 1), 0)
    wide_row = lax.broadcasted_iota(jnp.int32, (ROWS, ROWS), 0)
    col = lax.broadcasted_iota(jnp.int32, (ROWS, ROWS), 1)
    lane = lax.broadcasted_iota(jnp.int32, (ROWS, PIECE), 1)
    start = first_token(info_ref, wide_row)
    for back in range(1, CONV):
        chosen = (col == wide_row - back) & (col >= start)
        moves_ref[back - 1] = jnp.where(chosen, 1.0, 0.0).astype(BF16)
    moves = [moves_ref[k] for k in range(CONV - 1)]
    total = conv_sum(state_ref[...], state_taps_ref[...], moves)
    head_ref[:, 2048:] = total[:HEAD]
    state = silu(total).astype(BF16)
    read_in = state[:, :STATE]
    reads_ref[0] = read_in
    reads_ref[1] = state[:, STATE:]
    step = jax.nn.softplus(step_raw_ref[...] + bias_ref[...])
    running = -jnp.exp(decay_ref[...]) * step
    reach = 1
    while reach < ROWS:
        running = running + jnp.where(row >= reach, pltpu.roll(running, reach, 0), 0.0)
        reach *= 2
    running_ref[...] = running
    rows_ref[0] = jnp.transpose(running)
    rows_ref[1] = jnp.transpose(step)
    copies = [
        fetch(reads_ref, reads_hbm, sem.at[0]),
        fetch(running_ref, running_hbm, sem.at[1]),
        fetch(rows_ref, rows_hbm, sem.at[2]),
    ]
    last = running[ROWS - 1 :]
    last_start = start[ROWS - 1 :, :1]
    tail = jnp.where(row >= last_start, jnp.exp(last - running), 0.0) * step
    final = jnp.where(last_start < 0, jnp.exp(last), 0.0)
    final = jnp.broadcast_to(final, (16, final.shape[1]))
    line = lax.broadcasted_iota(jnp.int32, (16, PIECE), 0)
    for n in range(8):
        cols = slice(n * 256, (n + 1) * 256)
        total = conv_sum(raw_ref[:, cols], taps_ref[:, cols], moves)
        head_ref[:, cols] = total[:HEAD]
        inner_ref[:, cols] = silu(total).astype(BF16)
        if n % 2 == 1:
            group = slice((n - 1) * 256, (n + 1) * 256)
            copies.append(fetch(inner_ref.at[:, group], inner_hbm.at[:, group], sem.at[3 + n // 2]))
    late = jnp.where(row >= HEAD, tail, 0.0)
    for j in range(CONTEXT):
        cols = slice(j * PIECE, (j + 1) * PIECE)
        tail_ref[:, cols] = spread_pair(tail[:HEAD], j, lane[:HEAD])
        weighted = (spread_pair(late, j, lane) * inner_ref[:, cols].astype(F32)).astype(BF16)
        piece_ref[j] = lax.dot_general(
            read_in, weighted, (((0,), (0,)), ((), ())), preferred_element_type=F32
        )
        decay = spread_pair(final, j, lane[:16])
        high = decay.astype(BF16).astype(F32)
        decays_ref[j] = jnp.where(line == 0, high, decay - high).astype(BF16)
    for copy in copies:
        copy.wait()


def edge_kernel(
    info_ref, rim_ref, head_ref, tail_ref, part_ref, decays_ref, taps_ref, state_taps_ref,
    inner_head_hbm, reads_head_hbm, piece_ref, inner_ref, reads_ref, sem,
):
    row = lax.broadcasted_iota(jnp.int32, (8, 1), 0)
    start = first_token(info_ref, row)
    rest = jnp.zeros((HEAD - 8, 2304), F32)
    edge = jnp.concatenate(
        [
            conv_edge(rim_ref[:, :2048], taps_ref[...], start, row),
            conv_edge(rim_ref[:, 2048:], state_taps_ref[...], start, row),
        ],
        axis=1,
    )
    full = silu(head_ref[...] + jnp.concatenate([edge, rest], axis=0)).astype(BF16)
    inner = full[:, :2048]
    inner_ref[...] = inner
    reads_ref[0] = full[:, 2048 : 2048 + STATE]
    reads_ref[1] = full[:, 2048 + STATE :]
    copies = [fetch(inner_ref, inner_head_hbm, sem.at[0]), fetch(reads_ref, reads_head_hbm, sem.at[1])]
    weighted = (tail_ref[...] * inner.astype(F32)).astype(BF16)
    more = lax.dot_general(
        full[:, 2048 : 2048 + STATE], weighted, (((0,), (0,)), ((), ())), preferred_element_type=F32
    )
    for j in range(CONTEXT):
        piece = part_ref[j] + more[:, j * PIECE : (j + 1) * PIECE]
        piece_ref[j, :STATE] = piece.astype(BF16)
        piece_ref[j, STATE:] = decays_ref[j]
    for copy in copies:
        copy.wait()


def within_kernel(
    info_ref, inner_hbm, reads_hbm, running_hbm, rows_hbm, inner_head_hbm, reads_head_hbm, skip_ref, within_ref,
    inner_ref, reads_ref, running_ref, rows_ref, sem,
):
    copies = [
        fetch(reads_hbm.at[:, HEAD:], reads_ref.at[:, HEAD:], sem.at[0]),
        fetch(running_hbm, running_ref, sem.at[1]),
        fetch(rows_hbm, rows_ref, sem.at[2]),
        fetch(inner_hbm.at[HEAD:], inner_ref.at[HEAD:], sem.at[3]),
        fetch(reads_head_hbm, reads_ref.at[:, :HEAD], sem.at[4]),
        fetch(inner_head_hbm, inner_ref.at[:HEAD], sem.at[5]),
    ]
    row = lax.broadcasted_iota(jnp.int32, (ROWS, ROWS), 0)
    col = lax.broadcasted_iota(jnp.int32, (ROWS, ROWS), 1)
    same = (col >= first_token(info_ref, row)) & (col <= row)
    lane = lax.broadcasted_iota(jnp.int32, (ROWS, PIECE), 1)
    for copy in copies:
        copy.wait()
    pairwise = lax.dot_general(
        reads_ref[1], reads_ref[0], (((1,), (1,)), ((), ())), preferred_element_type=F32
    )
    pairwise = jnp.where(same, pairwise, 0.0)
    for j in range(CONTEXT):
        cols = slice(j * PIECE, (j + 1) * PIECE)
        inner = inner_ref[:, cols]
        parts = []
        for half in range(2):
            h = 2 * j + half
            gap = running_ref[:, h : h + 1] - rows_ref[0, h : h + 1, :]
            decay = jnp.exp(jnp.minimum(gap, 0.0))
            mixing = (decay * pairwise * rows_ref[1, h : h + 1, :]).astype(BF16)
            parts.append(jnp.dot(mixing, inner, preferred_element_type=F32))
        both = jnp.where(lane < 64, parts[0], parts[1])
        within_ref[:, cols] = both + skip_ref[:, cols] * inner.astype(F32)


def scan_kernel(piece_ref, after_ref, out_ref):
    carried = jnp.zeros((STATE, PIECE), F32)
    for k in range(CONTEXT):
        out_ref[k] = carried.astype(BF16)
        decay = piece_ref[k, STATE : STATE + 1, :].astype(F32) + piece_ref[k, STATE + 1 : STATE + 2, :].astype(F32)
        carried = decay * carried + piece_ref[k, :STATE, :].astype(F32)


def finish_kernel(
    info_ref, within_ref, gate_ref, reads_hbm, reads_head_hbm, running_hbm, carried_hbm, gated_ref, square_ref,
    read_ref, running_ref, carried_ref, sem,
):
    copies = [
        fetch(running_hbm, running_ref, sem.at[0]),
        fetch(reads_hbm.at[1, HEAD:], read_ref.at[HEAD:], sem.at[1]),
        fetch(reads_head_hbm.at[1], read_ref.at[:HEAD], sem.at[6]),
    ]
    for n in range(4):
        fetch(carried_hbm.at[4 * n : 4 * n + 4], carried_ref.at[4 * n : 4 * n + 4], sem.at[2 + n])
    row = lax.broadcasted_iota(jnp.int32, (ROWS, 1), 0)
    lane = lax.broadcasted_iota(jnp.int32, (ROWS, PIECE), 1)
    open_row = first_token(info_ref, row) < 0
    for copy in copies:
        copy.wait()
    entry = jnp.where(open_row, jnp.exp(running_ref[...]), 0.0)
    read_out = read_ref[...]
    squares = jnp.zeros((ROWS, PIECE), F32)
    for j in range(CONTEXT):
        cols = slice(j * PIECE, (j + 1) * PIECE)
        if j % 4 == 0:
            part = slice(j, j + 4)
            pltpu.make_async_copy(carried_hbm.at[part], carried_ref.at[part], sem.at[2 + j // 4]).wait()
        carried = jnp.dot(read_out, carried_ref[j], preferred_element_type=F32)
        ssm = within_ref[:, cols] + carried * spread_pair(entry, j, lane)
        gate = gate_ref[:, cols].astype(F32)
        gated = ssm * (gate * jax.nn.sigmoid(gate))
        gated_ref[:, cols] = gated
        squares = squares + gated * gated
    square_ref[...] = jnp.sum(jnp.transpose(squares), axis=0, keepdims=True)


def per_device(
    queries,
    key_states,
    value_states,
    segment_ids,
    hidden,
    attn_out_weight,
    norm_gain,
    gate_weight,
    inner_weight,
    state_proj_weight,
    step_weight,
    conv_inner,
    conv_state,
    step_bias,
    decay_log,
    skip_gain,
    out_gain,
):
    heads = step_weight.shape[1]
    dma = pltpu.SemaphoreType.DMA
    own, info = call(
        pack_kernel,
        [("v", (ROWS, 512), BF16), ("s", (8,), jnp.int32)],
        "hhh",
        [pltpu.VMEM((32, 128), jnp.int32), dma((3,))],
        4,
    )(key_states, value_states, segment_ids.reshape(32, 128))
    other_weight = swapped(attn_out_weight)
    attended, inner_near, own_near, other_near = attend(
        info, queries, own, inner_weight, attn_out_weight, other_weight
    )
    other = swapped(attended)
    mine = call(
        own_part_kernel, [("v", (ROWS, 2048), F32)], "vv", (), 8, 1_100_000_000, 4 << 20
    )(attended, own_near)
    residual, normed, inner_raw, state_raw, step_raw, rim = call(
        token_kernel,
        [
            ("h", (ROWS, 2048), BF16),
            ("h", (ROWS, 2048), BF16),
            ("v", (ROWS, 2048), BF16),
            ("v", (ROWS, 256), BF16),
            ("v", (ROWS, heads), F32),
            ("v", (8, 2304), BF16),
        ],
        "vvvhvvhv",
        [
            pltpu.VMEM((ROWS, 2048), BF16),
            pltpu.VMEM((2048, 256), BF16),
            pltpu.VMEM((ROWS, 2048), F32),
            pltpu.VMEM((ROWS, 2048), BF16),
            pltpu.VMEM((ROWS, 2048), BF16),
            dma((4,)),
        ],
        16,
        3_600_000_000,
        14 << 20,
    )(other, other_near, mine, hidden, norm_gain[None, :], inner_near, state_proj_weight, step_weight.T)
    rim = moved(rim, [(i, i + 1) for i in range(CONTEXT - 1)])
    buffers = [
        pltpu.VMEM((ROWS, 2048), BF16),
        pltpu.VMEM((2, ROWS, STATE), BF16),
        pltpu.VMEM((ROWS, heads), F32),
        pltpu.VMEM((2, heads, ROWS), F32),
    ]
    inner, reads, running, rows, part, decays, head, tail = call(
        prepare_kernel,
        [
            ("h", (ROWS, 2048), BF16),
            ("h", (2, ROWS, STATE), BF16),
            ("h", (ROWS, heads), F32),
            ("h", (2, heads, ROWS), F32),
            ("v", (CONTEXT, STATE, PIECE), F32),
            ("v", (CONTEXT, 16, PIECE), BF16),
            ("v", (HEAD, 2304), F32),
            ("v", (HEAD, 2048), F32),
        ],
        "svvvvvvv",
        buffers + [pltpu.VMEM((CONV - 1, ROWS, ROWS), BF16), dma((7,))],
        16,
        1_000_000_000,
        3 << 20,
    )(info, inner_raw, state_raw, step_raw, step_bias[None, :], decay_log[None, :], conv_inner, conv_state)
    inner_head, reads_head, pieces = call(
        edge_kernel,
        [
            ("h", (HEAD, 2048), BF16),
            ("h", (2, HEAD, STATE), BF16),
            ("v", (CONTEXT, PIECE_ROWS, PIECE), BF16),
        ],
        "svvvvvvv",
        [pltpu.VMEM((HEAD, 2048), BF16), pltpu.VMEM((2, HEAD, STATE), BF16), dma((2,))],
        8,
        10_000_000,
        2 << 20,
    )(info, rim, head, tail, part, decays, conv_inner, conv_state)
    gathered = lax.all_to_all(pieces, "context", 0, 0, tiled=True)
    skip = jnp.repeat(skip_gain, 64)[None, :]
    within = call(
        within_kernel,
        [("v", (ROWS, 2048), F32)],
        "shhhhhhv",
        buffers + [dma((6,))],
        16,
        3_000_000_000,
        4 << 20,
    )(info, inner, reads, running, rows, inner_head, reads_head, skip)
    carried = call(
        scan_kernel, [("v", (CONTEXT, STATE, PIECE), BF16)], "va", (), 8, 1_000_000, 1 << 20
    )(gathered, within)
    gate = call(
        gate_kernel,
        [("v", (ROWS, 2048), BF16)],
        "hha",
        [pltpu.VMEM((ROWS, 2048), BF16), pltpu.VMEM((2048, 2048), BF16), dma((5,))],
        20,
        2_200_000_000,
        9 << 20,
    )(normed, gate_weight, carried)
    carried = lax.all_to_all(carried, "context", 0, 0, tiled=True)
    gated, squares = call(
        finish_kernel,
        [("v", (ROWS, 2048), F32), ("v", (1, ROWS), F32)],
        "svvhhha",
        [
            pltpu.VMEM((ROWS, STATE), BF16),
            pltpu.VMEM((ROWS, heads), F32),
            pltpu.VMEM((CONTEXT, STATE, PIECE), BF16),
            dma((7,)),
        ],
        16,
        1_000_000_000,
        6 << 20,
    )(info, within, gate, reads, reads_head, running, carried)
    mixed = call(
        scale_kernel, [("v", (ROWS, 2048), BF16)], "vvvv", (), 8, 2_000_000, 3 << 20
    )(gated, squares, swapped(squares), out_gain[None, :])
    return (residual, mixed)


def solution(mesh):
    in_specs = (
        P(("seq", "context"), "tensor"),
        P(("seq", "context"), "tensor"),
        P(("seq", "context"), "tensor"),
        P("seq"),
        P(("seq", "context"), None),
        P("tensor", None),
        P(),
        P(None, "tensor"),
        P(None, "tensor"),
        P(),
        P(None, "tensor"),
        P(None, "tensor"),
        P(),
        P("tensor"),
        P("tensor"),
        P("tensor"),
        P("tensor"),
    )
    out_specs = (P(("seq", "context"), None), P(("seq", "context"), "tensor"))
    return jax.shard_map(
        per_device, mesh=mesh, in_specs=in_specs, out_specs=out_specs, check_vma=False
    )
```

```python
import functools
import jax
import jax.numpy as jnp
from jax import lax
from jax.experimental import pallas as pl
from jax.experimental.pallas import tpu as pltpu
from jax.sharding import PartitionSpec as P

ATT_HEADS = 16
KV_HEADS = 4
HEAD_DIM = 128
STATE = 128
CONV = 4
WINDOW = 2048
D_INNER = 4096
ROWS = 256
REACH = 8
CONTEXT = 16
PIECE = 128
PIECE_ROWS = STATE + 16
HEAD = 16
EPSILON = 1e-05
NEG = -1e30
LOG2E = 1.4426950408889634


F32 = jnp.float32
BF16 = jnp.bfloat16


def moved(x, pairs):
    return lax.ppermute(x, "context", pairs)


def swapped(x):
    return lax.ppermute(x, "tensor", [(0, 1), (1, 0)])


def call(kernel, outs, ins, scratch=(), limit=16, flops=0, bytes_accessed=0, flags=None):
    space = {"v": pltpu.VMEM, "s": pltpu.SMEM, "h": pltpu.HBM, "a": pl.ANY}
    single = len(outs) == 1
    shapes = tuple(
        pltpu.HBM(o[1], o[2]) if o[0] == "h" else jax.ShapeDtypeStruct(o[1], o[2]) for o in outs
    )
    specs = tuple(pl.BlockSpec(memory_space=space[o[0]]) for o in outs)
    run = pl.pallas_call(
        kernel,
        out_shape=shapes[0] if single else shapes,
        in_specs=[pl.BlockSpec(memory_space=space[k]) for k in ins],
        out_specs=specs[0] if single else specs,
        scratch_shapes=list(scratch),
        compiler_params=pltpu.CompilerParams(vmem_limit_bytes=limit << 20, flags=flags),
        cost_estimate=pl.CostEstimate(flops=flops, bytes_accessed=bytes_accessed, transcendentals=0),
    )

    def placed(*operands):
        return run(
            *(pltpu.with_memory_space_constraint(x, pltpu.HBM) if k == "h" else x for x, k in zip(operands, ins))
        )

    return placed


def fetch(source, target, semaphore):
    copy = pltpu.make_async_copy(source, target, semaphore)
    copy.start()
    return copy


def columns(n):
    return pl.ds(pl.multiple_of(n * 512, 512), 512)


def first_token(info_ref, row):
    start = info_ref[3]
    for v in range(3):
        start = jnp.maximum(start, jnp.where(info_ref[v] <= row, info_ref[v], info_ref[3]))
    return start


def pack_kernel(key_ref, value_ref, seg_ref, own_ref, info_ref, seg_v, sem):
    copies = [
        fetch(seg_ref, seg_v, sem.at[2]),
        fetch(key_ref, own_ref.at[:, :256], sem.at[0]),
        fetch(value_ref, own_ref.at[:, 256:], sem.at[1]),
    ]
    copies[0].wait()
    place = lax.axis_index("context")
    anchor = place * ROWS
    for v in range(3):
        below = jnp.where(seg_v[...] <= v, 1.0, 0.0)
        info_ref[v] = jnp.sum(below).astype(jnp.int32) - anchor
    info_ref[3] = -anchor
    info_ref[4] = lax.rem(place, 4)
    copies[1].wait()
    copies[2].wait()


def block_bias(place, lower):
    return jnp.where(place >= lower, 0.0, NEG)


def attend_pairs(q_ref, block_ref, n, bias_ref, s_refs, p_refs, carry_in, finish):
    scale = HEAD_DIM ** (-0.5) * LOG2E
    wide = n * ROWS
    chunk = 32
    ones = jnp.ones((wide, 128), BF16)

    def group(g, carry):
        at = pl.multiple_of(g * 128, 128)
        keys = block_ref[:, :, pl.ds(at, 128)].reshape(wide, 128)
        for half in range(2):
            from_col = pl.multiple_of(g * 512 + half * 256, 256)
            both = q_ref[:, pl.ds(from_col, 256)]
            q = jnp.concatenate([both[:, :128], both[:, 128:]], axis=0)
            s_refs[half][...] = lax.dot_general(
                q, keys, (((1,), (1,)), ((), ())), preferred_element_type=F32
            )
        values = block_ref[:, :, pl.ds(pl.multiple_of(at + 256, 128), 128)].reshape(wide, 128)
        values = jnp.concatenate([values, ones], axis=1)
        for half in range(2):
            index = 2 * g + half
            for c in range(2 * ROWS // chunk):
                rows = slice(c * chunk, (c + 1) * chunk)
                from_row = (c * chunk) % ROWS
                s = s_refs[half][rows] * scale + bias_ref[from_row : from_row + chunk]
                top = jnp.max(s, axis=-1, keepdims=True)
                if carry_in is not None:
                    before = carry_in[3][index, rows]
                    top = jnp.maximum(top, before)
                    alpha = jnp.exp2(before - top)
                    carry_in[0][index, rows] = alpha
                    top = top[:, :1]
                p_refs[half][rows] = jnp.exp2(s - top).astype(BF16)
                if carry_in is None:
                    finish[0][index, rows] = jnp.broadcast_to(top, (chunk, 128))
            both = jnp.dot(p_refs[half][...], values, preferred_element_type=F32)
            blended, total = both[:, :128], both[:, 128:]
            if carry_in is None:
                finish[1][index] = total
                finish[2][index] = blended
            else:
                alpha = carry_in[0][index]
                total = total + alpha * carry_in[1][index]
                blended = ((blended + alpha * carry_in[2][index]) / total).astype(BF16)
                finish[:, pl.ds(pl.multiple_of(index * 256, 256), 256)] = jnp.concatenate(
                    [blended[:ROWS], blended[ROWS:]], axis=1
                )
        return carry

    lax.fori_loop(0, 2, group, 0)


def attend_scratch(n, extra=()):
    return [
        pltpu.VMEM((ROWS, n * ROWS), F32),
        pltpu.VMEM((n, ROWS, 512), BF16),
        pltpu.VMEM((ROWS, 1024), BF16),
        pltpu.VMEM((2 * ROWS, n * ROWS), F32),
        pltpu.VMEM((2 * ROWS, n * ROWS), F32),
        pltpu.VMEM((2 * ROWS, n * ROWS), BF16),
        pltpu.VMEM((2 * ROWS, n * ROWS), BF16),
        *extra,
        pltpu.SemaphoreType.DMA((n + 1,)),
    ]


def attend_first_kernel(
    info_ref, q_hbm, own_ref, y1_hbm, y2_hbm, weight_hbm,
    top_ref, total_ref, sum_ref, weight_ref,
    bias_ref, block_ref, q_ref, s0, s1, e0, e1, weight_sem, sem,
):
    copies = [fetch(q_hbm, q_ref, sem.at[3])]
    for k, source in enumerate((own_ref, y1_hbm, y2_hbm)):
        copies.append(fetch(source, block_ref.at[k], sem.at[k]))
    row = lax.broadcasted_iota(jnp.int32, (ROWS, ROWS), 0)
    col = lax.broadcasted_iota(jnp.int32, (ROWS, ROWS), 1)
    lower = jnp.maximum(first_token(info_ref, row), row - (WINDOW - 1))
    bias_ref[:, :ROWS] = jnp.where((col >= lower) & (col <= row), 0.0, NEG)
    bias_ref[:, ROWS : 2 * ROWS] = block_bias(col - 4 * ROWS, lower)
    bias_ref[:, 2 * ROWS :] = block_bias(col - 8 * ROWS, lower)
    for copy in copies:
        copy.wait()
    weight = fetch(weight_hbm, weight_ref, weight_sem)
    attend_pairs(q_ref, block_ref, 3, bias_ref, (s0, s1), (e0, e1), None, (top_ref, total_ref, sum_ref))
    weight.wait()


def attend_rest_kernel(
    info_ref, q_hbm, p1, p2, p3, w1, w2, w3, r1, r2, r3, top_ref, total_ref, sum_ref, other_hbm, own_hbm,
    out_ref, other_ref, own_ref,
    bias_ref, block_ref, q_ref, s0, s1, e0, e1, alpha_ref, weight_sem, sem,
):
    z = info_ref[4]
    copies = [fetch(q_hbm, q_ref, sem.at[6])]
    for s, (p, w) in enumerate(((p1, w1), (p2, w2), (p3, w3))):

        @pl.when(z >= s + 1)
        def _():
            pltpu.make_async_copy(p, block_ref.at[s], sem.at[s]).start()

        @pl.when(z < s + 1)
        def _():
            pltpu.make_async_copy(w, block_ref.at[s], sem.at[s]).start()

    for s, r in enumerate((r1, r2, r3)):
        copies.append(fetch(r, block_ref.at[3 + s], sem.at[3 + s]))
    row = lax.broadcasted_iota(jnp.int32, (ROWS, 1), 0)
    col = lax.broadcasted_iota(jnp.int32, (ROWS, ROWS), 1)
    lower = jnp.maximum(first_token(info_ref, row), row - (WINDOW - 1))
    for s in range(3):
        near = z >= s + 1
        bias_ref[:, s * ROWS : (s + 1) * ROWS] = block_bias(col - jnp.where(near, s + 1, s + 5) * ROWS, lower)
        bias_ref[:, (s + 3) * ROWS : (s + 4) * ROWS] = block_bias(
            col - jnp.where(near, s + 5, s + 1) * ROWS, lower
        )
    for copy in copies:
        copy.wait()
    for s in range(3):
        pltpu.make_async_copy(p1, block_ref.at[s], sem.at[s]).wait()
    weights = [
        fetch(own_hbm, own_ref, weight_sem.at[0]),
        fetch(other_hbm, other_ref, weight_sem.at[1]),
    ]
    attend_pairs(
        q_ref, block_ref, 6, bias_ref, (s0, s1), (e0, e1), (alpha_ref, total_ref, sum_ref, top_ref), out_ref
    )
    for weight in weights:
        weight.wait()


def attend(info, queries, own, inner_weight, own_weight, other_weight):
    near = range(4)
    y1 = moved(own, [(4 * y + x, 4 * y + 4 + x) for y in range(3) for x in near])
    y2 = moved(own, [(4 * y + x, 4 * y + 8 + x) for y in range(2) for x in near])
    p = [moved(own, [(4 * y + x, 4 * y + x + s) for y in near for x in near if x + s < 4]) for s in (1, 2, 3)]
    r = [moved(y1, [(4 * y + x, 4 * y + (x + s) % 4) for y in (1, 2, 3) for x in near]) for s in (1, 2, 3)]
    p[1] = moved(own, [(4 * y + x, 4 * y + (x + 2) % 4) for y in near for x in near])
    r[1] = moved(p[1], [(4 * y + x, 4 * y + 4 + x) for y in range(3) for x in near])
    w = [moved(y2, [(4 * y + x, 4 * y + x + s - 4) for y in (2, 3) for x in near if x + s >= 4]) for s in (1, 2, 3)]
    part = ("v", (4, 2 * ROWS, 128), F32)
    one = pltpu.SemaphoreType.DMA
    *carry, inner_near = call(
        attend_first_kernel,
        [part] * 3 + [("v", (2048, 2048), BF16)],
        "shaaah",
        attend_scratch(3, [one]),
        20,
        1_600_000_000,
        4 << 20,
    )(info, queries, own, y1, y2, inner_weight)
    attended, other_near, own_near = call(
        attend_rest_kernel,
        [("v", (ROWS, 1024), BF16), ("v", (1024, 2048), BF16), ("v", (1024, 2048), BF16)],
        "sh" + "a" * 9 + "vvvah",
        attend_scratch(6, [pltpu.VMEM((4, 2 * ROWS, 128), F32), pltpu.SemaphoreType.DMA((2,))]),
        32,
        3_400_000_000,
        4 << 20,
    )(info, queries, *p, *w, *r, *carry, other_weight, own_weight)
    return attended, inner_near, own_near, other_near


def own_part_kernel(x_ref, w_ref, out_ref):
    for n in range(4):
        cols = slice(n * 512, n * 512 + 512)
        out_ref[:, cols] = jnp.dot(x_ref[...], w_ref[:, cols], preferred_element_type=F32)


def token_kernel(
    x_ref, w_ref, mine_ref, hidden_hbm, gain_ref, inner_ref, state_hbm, step_ref,
    residual_hbm, normed_hbm, raw_ref, state_out_ref, step_out_ref, rim_ref,
    hidden_ref, state_ref, theirs_ref, residual_ref, normed_ref, sem,
):
    hidden = fetch(hidden_hbm, hidden_ref, sem.at[0])
    state = fetch(state_hbm, state_ref, sem.at[1])
    theirs_ref[:, :512] = jnp.dot(x_ref[...], w_ref[:, :512], preferred_element_type=F32)
    hidden.wait()
    squares = jnp.zeros((ROWS, 128), F32)
    for n in range(4):
        cols = slice(n * 512, n * 512 + 512)
        if n > 0:
            theirs_ref[:, cols] = jnp.dot(x_ref[...], w_ref[:, cols], preferred_element_type=F32)
        total = hidden_ref[:, cols].astype(F32) + (mine_ref[:, cols] + theirs_ref[:, cols])
        low = total.astype(BF16)
        residual_ref[:, cols] = low
        wide = low.astype(F32)
        wide = wide * wide
        squares = squares + (wide[:, :128] + wide[:, 128:256]) + (wide[:, 256:384] + wide[:, 384:])
    residual = fetch(residual_ref, residual_hbm, sem.at[2])
    mean = jnp.sum(squares, axis=-1, keepdims=True) * (1.0 / 2048.0)
    scale = lax.rsqrt(mean + EPSILON)
    for n in range(4):
        cols = slice(n * 512, (n + 1) * 512)
        normed_ref[:, cols] = (
            residual_ref[:, cols].astype(F32) * scale * gain_ref[:, cols].astype(F32)
        ).astype(BF16)
    normed = fetch(normed_ref, normed_hbm, sem.at[3])
    state.wait()
    narrow = jnp.dot(normed_ref[...], state_ref[...], preferred_element_type=F32).astype(BF16)
    state_out_ref[...] = narrow
    rim_ref[:, 2048:] = narrow[ROWS - 8 :]
    step_out_ref[...] = lax.dot_general(
        normed_ref[...], step_ref[...], (((1,), (1,)), ((), ())), preferred_element_type=F32
    )

    def in_tile(n, carry):
        cols = columns(n)
        raw = jnp.dot(normed_ref[...], inner_ref[:, cols], preferred_element_type=F32).astype(BF16)
        raw_ref[:, cols] = raw
        rim_ref[:, cols] = raw[ROWS - 8 :]
        return carry

    lax.fori_loop(0, 4, in_tile, 0)
    residual.wait()
    normed.wait()


def gate_kernel(x_hbm, w_hbm, after_ref, out_ref, x_ref, w_ref, sem):
    first = fetch(x_hbm, x_ref, sem.at[4])
    for n in range(4):
        fetch(w_hbm.at[:, n * 512 : n * 512 + 512], w_ref.at[:, n * 512 : n * 512 + 512], sem.at[n])
    first.wait()

    def tile(n, carry):
        cols = columns(n)
        pltpu.make_async_copy(w_hbm.at[:, cols], w_ref.at[:, cols], sem.at[n]).wait()
        out_ref[:, cols] = jnp.dot(x_ref[...], w_ref[:, cols], preferred_element_type=F32).astype(BF16)
        return carry

    lax.fori_loop(0, 4, tile, 0)


def scale_kernel(gated_ref, mine_ref, theirs_ref, gain_ref, out_ref):
    squares = jnp.broadcast_to(mine_ref[...] + theirs_ref[...], (128, ROWS))
    scale = lax.rsqrt(jnp.transpose(squares) * (1.0 / D_INNER) + EPSILON)
    for j in range(CONTEXT):
        cols = slice(j * PIECE, (j + 1) * PIECE)
        out_ref[:, cols] = (gated_ref[:, cols] * scale * gain_ref[:, cols].astype(F32)).astype(BF16)


def conv_sum(raw, taps, moves):
    taps = taps.astype(F32)
    total = raw.astype(F32) * taps[CONV - 1 : CONV]
    for back in range(1, CONV):
        tap = taps[CONV - 1 - back : CONV - back]
        total = total + jnp.dot(moves[back - 1], raw, preferred_element_type=F32) * tap
    return total


def conv_edge(rim, taps, start, row):
    early = rim.astype(F32)
    taps = taps.astype(F32)
    edge = jnp.zeros_like(early)
    for back in range(1, CONV):
        tap = taps[CONV - 1 - back : CONV - back]
        keep = (row < back) & (row - back >= start)
        edge = edge + jnp.where(keep, pltpu.roll(early, back, 0) * tap, 0.0)
    return edge


def silu(x):
    return x * jax.nn.sigmoid(x)


def spread_pair(values, j, lane):
    return jnp.where(lane < 64, values[:, 2 * j : 2 * j + 1], values[:, 2 * j + 1 : 2 * j + 2])


def prepare_kernel(
    info_ref, raw_ref, state_ref, step_raw_ref, bias_ref, decay_ref, taps_ref, state_taps_ref,
    inner_hbm, reads_hbm, running_hbm, rows_hbm, piece_ref, decays_ref, head_ref, tail_ref,
    inner_ref, reads_ref, running_ref, rows_ref, moves_ref, sem,
):
    row = lax.broadcasted_iota(jnp.int32, (ROWS, 1), 0)
    wide_row = lax.broadcasted_iota(jnp.int32, (ROWS, ROWS), 0)
    col = lax.broadcasted_iota(jnp.int32, (ROWS, ROWS), 1)
    lane = lax.broadcasted_iota(jnp.int32, (ROWS, PIECE), 1)
    start = first_token(info_ref, wide_row)
    for back in range(1, CONV):
        chosen = (col == wide_row - back) & (col >= start)
        moves_ref[back - 1] = jnp.where(chosen, 1.0, 0.0).astype(BF16)
    moves = [moves_ref[k] for k in range(CONV - 1)]
    total = conv_sum(state_ref[...], state_taps_ref[...], moves)
    head_ref[:, 2048:] = total[:HEAD]
    state = silu(total).astype(BF16)
    read_in = state[:, :STATE]
    reads_ref[0] = read_in
    reads_ref[1] = state[:, STATE:]
    step = jax.nn.softplus(step_raw_ref[...] + bias_ref[...])
    running = -jnp.exp(decay_ref[...]) * step
    reach = 1
    while reach < ROWS:
        running = running + jnp.where(row >= reach, pltpu.roll(running, reach, 0), 0.0)
        reach *= 2
    running_ref[...] = running
    rows_ref[0] = jnp.transpose(running)
    rows_ref[1] = jnp.transpose(step)
    copies = [
        fetch(reads_ref, reads_hbm, sem.at[0]),
        fetch(running_ref, running_hbm, sem.at[1]),
        fetch(rows_ref, rows_hbm, sem.at[2]),
    ]
    last = running[ROWS - 1 :]
    last_start = start[ROWS - 1 :, :1]
    tail = jnp.where(row >= last_start, jnp.exp(last - running), 0.0) * step
    final = jnp.where(last_start < 0, jnp.exp(last), 0.0)
    final = jnp.broadcast_to(final, (16, final.shape[1]))
    line = lax.broadcasted_iota(jnp.int32, (16, PIECE), 0)
    for n in range(8):
        cols = slice(n * 256, (n + 1) * 256)
        total = conv_sum(raw_ref[:, cols], taps_ref[:, cols], moves)
        head_ref[:, cols] = total[:HEAD]
        inner_ref[:, cols] = silu(total).astype(BF16)
        if n % 2 == 1:
            group = slice((n - 1) * 256, (n + 1) * 256)
            copies.append(fetch(inner_ref.at[:, group], inner_hbm.at[:, group], sem.at[3 + n // 2]))
    late = jnp.where(row >= HEAD, tail, 0.0)
    for j in range(CONTEXT):
        cols = slice(j * PIECE, (j + 1) * PIECE)
        tail_ref[:, cols] = spread_pair(tail[:HEAD], j, lane[:HEAD])
        weighted = (spread_pair(late, j, lane) * inner_ref[:, cols].astype(F32)).astype(BF16)
        piece_ref[j] = lax.dot_general(
            read_in, weighted, (((0,), (0,)), ((), ())), preferred_element_type=F32
        )
        decay = spread_pair(final, j, lane[:16])
        high = decay.astype(BF16).astype(F32)
        decays_ref[j] = jnp.where(line == 0, high, decay - high).astype(BF16)
    for copy in copies:
        copy.wait()


def edge_kernel(
    info_ref, rim_ref, head_ref, tail_ref, part_ref, decays_ref, taps_ref, state_taps_ref,
    inner_head_hbm, reads_head_hbm, piece_ref, inner_ref, reads_ref, sem,
):
    row = lax.broadcasted_iota(jnp.int32, (8, 1), 0)
    start = first_token(info_ref, row)
    rest = jnp.zeros((HEAD - 8, 2304), F32)
    edge = jnp.concatenate(
        [
            conv_edge(rim_ref[:, :2048], taps_ref[...], start, row),
            conv_edge(rim_ref[:, 2048:], state_taps_ref[...], start, row),
        ],
        axis=1,
    )
    full = silu(head_ref[...] + jnp.concatenate([edge, rest], axis=0)).astype(BF16)
    inner = full[:, :2048]
    inner_ref[...] = inner
    reads_ref[0] = full[:, 2048 : 2048 + STATE]
    reads_ref[1] = full[:, 2048 + STATE :]
    copies = [fetch(inner_ref, inner_head_hbm, sem.at[0]), fetch(reads_ref, reads_head_hbm, sem.at[1])]
    weighted = (tail_ref[...] * inner.astype(F32)).astype(BF16)
    more = lax.dot_general(
        full[:, 2048 : 2048 + STATE], weighted, (((0,), (0,)), ((), ())), preferred_element_type=F32
    )
    for j in range(CONTEXT):
        piece = part_ref[j] + more[:, j * PIECE : (j + 1) * PIECE]
        piece_ref[j, :STATE] = piece.astype(BF16)
        piece_ref[j, STATE:] = decays_ref[j]
    for copy in copies:
        copy.wait()


def within_kernel(
    info_ref, inner_hbm, reads_hbm, running_hbm, rows_hbm, inner_head_hbm, reads_head_hbm, skip_ref, within_ref,
    inner_ref, reads_ref, running_ref, rows_ref, sem,
):
    copies = [
        fetch(reads_hbm.at[:, HEAD:], reads_ref.at[:, HEAD:], sem.at[0]),
        fetch(running_hbm, running_ref, sem.at[1]),
        fetch(rows_hbm, rows_ref, sem.at[2]),
        fetch(inner_hbm.at[HEAD:], inner_ref.at[HEAD:], sem.at[3]),
        fetch(reads_head_hbm, reads_ref.at[:, :HEAD], sem.at[4]),
        fetch(inner_head_hbm, inner_ref.at[:HEAD], sem.at[5]),
    ]
    row = lax.broadcasted_iota(jnp.int32, (ROWS, ROWS), 0)
    col = lax.broadcasted_iota(jnp.int32, (ROWS, ROWS), 1)
    same = (col >= first_token(info_ref, row)) & (col <= row)
    lane = lax.broadcasted_iota(jnp.int32, (ROWS, PIECE), 1)
    for copy in copies:
        copy.wait()
    pairwise = lax.dot_general(
        reads_ref[1], reads_ref[0], (((1,), (1,)), ((), ())), preferred_element_type=F32
    )
    pairwise = jnp.where(same, pairwise, 0.0)
    for j in range(CONTEXT):
        cols = slice(j * PIECE, (j + 1) * PIECE)
        inner = inner_ref[:, cols]
        parts = []
        for half in range(2):
            h = 2 * j + half
            gap = running_ref[:, h : h + 1] - rows_ref[0, h : h + 1, :]
            decay = jnp.exp(jnp.minimum(gap, 0.0))
            mixing = (decay * pairwise * rows_ref[1, h : h + 1, :]).astype(BF16)
            parts.append(jnp.dot(mixing, inner, preferred_element_type=F32))
        both = jnp.where(lane < 64, parts[0], parts[1])
        within_ref[:, cols] = both + skip_ref[:, cols] * inner.astype(F32)


def scan_kernel(piece_ref, after_ref, out_ref):
    carried = jnp.zeros((STATE, PIECE), F32)
    for k in range(CONTEXT):
        out_ref[k] = carried.astype(BF16)
        decay = piece_ref[k, STATE : STATE + 1, :].astype(F32) + piece_ref[k, STATE + 1 : STATE + 2, :].astype(F32)
        carried = decay * carried + piece_ref[k, :STATE, :].astype(F32)


def finish_kernel(
    info_ref, within_ref, gate_ref, reads_hbm, reads_head_hbm, running_hbm, carried_hbm, gated_ref, square_ref,
    read_ref, running_ref, carried_ref, sem,
):
    copies = [
        fetch(running_hbm, running_ref, sem.at[0]),
        fetch(reads_hbm.at[1, HEAD:], read_ref.at[HEAD:], sem.at[1]),
        fetch(reads_head_hbm.at[1], read_ref.at[:HEAD], sem.at[6]),
    ]
    for n in range(4):
        fetch(carried_hbm.at[4 * n : 4 * n + 4], carried_ref.at[4 * n : 4 * n + 4], sem.at[2 + n])
    row = lax.broadcasted_iota(jnp.int32, (ROWS, 1), 0)
    lane = lax.broadcasted_iota(jnp.int32, (ROWS, PIECE), 1)
    open_row = first_token(info_ref, row) < 0
    for copy in copies:
        copy.wait()
    entry = jnp.where(open_row, jnp.exp(running_ref[...]), 0.0)
    read_out = read_ref[...]
    squares = jnp.zeros((ROWS, PIECE), F32)
    for j in range(CONTEXT):
        cols = slice(j * PIECE, (j + 1) * PIECE)
        if j % 4 == 0:
            part = slice(j, j + 4)
            pltpu.make_async_copy(carried_hbm.at[part], carried_ref.at[part], sem.at[2 + j // 4]).wait()
        carried = jnp.dot(read_out, carried_ref[j], preferred_element_type=F32)
        ssm = within_ref[:, cols] + carried * spread_pair(entry, j, lane)
        gate = gate_ref[:, cols].astype(F32)
        gated = ssm * (gate * jax.nn.sigmoid(gate))
        gated_ref[:, cols] = gated
        squares = squares + gated * gated
    square_ref[...] = jnp.sum(jnp.transpose(squares), axis=0, keepdims=True)


def per_device(
    queries,
    key_states,
    value_states,
    segment_ids,
    hidden,
    attn_out_weight,
    norm_gain,
    gate_weight,
    inner_weight,
    state_proj_weight,
    step_weight,
    conv_inner,
    conv_state,
    step_bias,
    decay_log,
    skip_gain,
    out_gain,
):
    heads = step_weight.shape[1]
    dma = pltpu.SemaphoreType.DMA
    own, info = call(
        pack_kernel,
        [("v", (ROWS, 512), BF16), ("s", (8,), jnp.int32)],
        "hhh",
        [pltpu.VMEM((32, 128), jnp.int32), dma((3,))],
        4,
    )(key_states, value_states, segment_ids.reshape(32, 128))
    other_weight = swapped(attn_out_weight)
    attended, inner_near, own_near, other_near = attend(
        info, queries, own, inner_weight, attn_out_weight, other_weight
    )
    other = swapped(attended)
    mine = call(
        own_part_kernel, [("v", (ROWS, 2048), F32)], "vv", (), 8, 1_100_000_000, 4 << 20
    )(attended, own_near)
    residual, normed, inner_raw, state_raw, step_raw, rim = call(
        token_kernel,
        [
            ("h", (ROWS, 2048), BF16),
            ("h", (ROWS, 2048), BF16),
            ("v", (ROWS, 2048), BF16),
            ("v", (ROWS, 256), BF16),
            ("v", (ROWS, heads), F32),
            ("v", (8, 2304), BF16),
        ],
        "vvvhvvhv",
        [
            pltpu.VMEM((ROWS, 2048), BF16),
            pltpu.VMEM((2048, 256), BF16),
            pltpu.VMEM((ROWS, 2048), F32),
            pltpu.VMEM((ROWS, 2048), BF16),
            pltpu.VMEM((ROWS, 2048), BF16),
            dma((4,)),
        ],
        16,
        3_600_000_000,
        14 << 20,
    )(other, other_near, mine, hidden, norm_gain[None, :], inner_near, state_proj_weight, step_weight.T)
    rim = moved(rim, [(i, i + 1) for i in range(CONTEXT - 1)])
    buffers = [
        pltpu.VMEM((ROWS, 2048), BF16),
        pltpu.VMEM((2, ROWS, STATE), BF16),
        pltpu.VMEM((ROWS, heads), F32),
        pltpu.VMEM((2, heads, ROWS), F32),
    ]
    inner, reads, running, rows, part, decays, head, tail = call(
        prepare_kernel,
        [
            ("h", (ROWS, 2048), BF16),
            ("h", (2, ROWS, STATE), BF16),
            ("h", (ROWS, heads), F32),
            ("h", (2, heads, ROWS), F32),
            ("v", (CONTEXT, STATE, PIECE), F32),
            ("v", (CONTEXT, 16, PIECE), BF16),
            ("v", (HEAD, 2304), F32),
            ("v", (HEAD, 2048), F32),
        ],
        "svvvvvvv",
        buffers + [pltpu.VMEM((CONV - 1, ROWS, ROWS), BF16), dma((7,))],
        16,
        1_000_000_000,
        3 << 20,
    )(info, inner_raw, state_raw, step_raw, step_bias[None, :], decay_log[None, :], conv_inner, conv_state)
    inner_head, reads_head, pieces = call(
        edge_kernel,
        [
            ("h", (HEAD, 2048), BF16),
            ("h", (2, HEAD, STATE), BF16),
            ("v", (CONTEXT, PIECE_ROWS, PIECE), BF16),
        ],
        "svvvvvvv",
        [pltpu.VMEM((HEAD, 2048), BF16), pltpu.VMEM((2, HEAD, STATE), BF16), dma((2,))],
        8,
        10_000_000,
        2 << 20,
    )(info, rim, head, tail, part, decays, conv_inner, conv_state)
    gathered = lax.all_to_all(pieces, "context", 0, 0, tiled=True)
    skip = jnp.repeat(skip_gain, 64)[None, :]
    within = call(
        within_kernel,
        [("v", (ROWS, 2048), F32)],
        "shhhhhhv",
        buffers + [dma((6,))],
        16,
        3_000_000_000,
        4 << 20,
    )(info, inner, reads, running, rows, inner_head, reads_head, skip)
    carried = call(
        scan_kernel, [("v", (CONTEXT, STATE, PIECE), BF16)], "va", (), 8, 1_000_000, 1 << 20
    )(gathered, within)
    gate = call(
        gate_kernel,
        [("v", (ROWS, 2048), BF16)],
        "hha",
        [pltpu.VMEM((ROWS, 2048), BF16), pltpu.VMEM((2048, 2048), BF16), dma((5,))],
        20,
        2_200_000_000,
        9 << 20,
    )(normed, gate_weight, carried)
    carried = lax.all_to_all(carried, "context", 0, 0, tiled=True)
    gated, squares = call(
        finish_kernel,
        [("v", (ROWS, 2048), F32), ("v", (1, ROWS), F32)],
        "svvhhha",
        [
            pltpu.VMEM((ROWS, STATE), BF16),
            pltpu.VMEM((ROWS, heads), F32),
            pltpu.VMEM((CONTEXT, STATE, PIECE), BF16),
            dma((7,)),
        ],
        16,
        1_000_000_000,
        6 << 20,
    )(info, within, gate, reads, reads_head, running, carried)
    mixed = call(
        scale_kernel, [("v", (ROWS, 2048), BF16)], "vvvv", (), 8, 2_000_000, 3 << 20
    )(gated, squares, swapped(squares), out_gain[None, :])
    return (residual, mixed)


def solution(mesh):
    in_specs = (
        P(("seq", "context"), "tensor"),
        P(("seq", "context"), "tensor"),
        P(("seq", "context"), "tensor"),
        P("seq"),
        P(("seq", "context"), None),
        P("tensor", None),
        P(),
        P(None, "tensor"),
        P(None, "tensor"),
        P(),
        P(None, "tensor"),
        P(None, "tensor"),
        P(),
        P("tensor"),
        P("tensor"),
        P("tensor"),
        P("tensor"),
    )
    out_specs = (P(("seq", "context"), None), P(("seq", "context"), "tensor"))
    return jax.shard_map(
        per_device, mesh=mesh, in_specs=in_specs, out_specs=out_specs, check_vma=False
    )
```

```python
import functools
import jax
import jax.numpy as jnp
from jax import lax
from jax.experimental import pallas as pl
from jax.experimental.pallas import tpu as pltpu
from jax.sharding import PartitionSpec as P

ATT_HEADS = 16
KV_HEADS = 4
HEAD_DIM = 128
STATE = 128
CONV = 4
WINDOW = 2048
D_INNER = 4096
ROWS = 256
REACH = 8
CONTEXT = 16
PIECE = 128
PIECE_ROWS = STATE + 16
HEAD = 16
EPSILON = 1e-05
NEG = -1e30
LOG2E = 1.4426950408889634


F32 = jnp.float32
BF16 = jnp.bfloat16


def moved(x, pairs):
    return lax.ppermute(x, "context", pairs)


def swapped(x):
    return lax.ppermute(x, "tensor", [(0, 1), (1, 0)])


def call(kernel, outs, ins, scratch=(), limit=16, flops=0, bytes_accessed=0, flags=None):
    space = {"v": pltpu.VMEM, "s": pltpu.SMEM, "h": pltpu.HBM, "a": pl.ANY}
    single = len(outs) == 1
    shapes = tuple(
        pltpu.HBM(o[1], o[2]) if o[0] == "h" else jax.ShapeDtypeStruct(o[1], o[2]) for o in outs
    )
    specs = tuple(pl.BlockSpec(memory_space=space[o[0]]) for o in outs)
    run = pl.pallas_call(
        kernel,
        out_shape=shapes[0] if single else shapes,
        in_specs=[pl.BlockSpec(memory_space=space[k]) for k in ins],
        out_specs=specs[0] if single else specs,
        scratch_shapes=list(scratch),
        compiler_params=pltpu.CompilerParams(vmem_limit_bytes=limit << 20, flags=flags),
        cost_estimate=pl.CostEstimate(flops=flops, bytes_accessed=bytes_accessed, transcendentals=0),
    )

    def placed(*operands):
        return run(
            *(pltpu.with_memory_space_constraint(x, pltpu.HBM) if k == "h" else x for x, k in zip(operands, ins))
        )

    return placed


def fetch(source, target, semaphore):
    copy = pltpu.make_async_copy(source, target, semaphore)
    copy.start()
    return copy


def columns(n):
    return pl.ds(pl.multiple_of(n * 512, 512), 512)


def first_token(info_ref, row):
    start = info_ref[3]
    for v in range(3):
        start = jnp.maximum(start, jnp.where(info_ref[v] <= row, info_ref[v], info_ref[3]))
    return start


def pack_kernel(key_ref, value_ref, seg_ref, own_ref, info_ref, seg_v, sem):
    copies = [
        fetch(seg_ref, seg_v, sem.at[2]),
        fetch(key_ref, own_ref.at[:, :256], sem.at[0]),
        fetch(value_ref, own_ref.at[:, 256:], sem.at[1]),
    ]
    copies[0].wait()
    place = lax.axis_index("context")
    anchor = place * ROWS
    for v in range(3):
        below = jnp.where(seg_v[...] <= v, 1.0, 0.0)
        info_ref[v] = jnp.sum(below).astype(jnp.int32) - anchor
    info_ref[3] = -anchor
    info_ref[4] = lax.rem(place, 4)
    copies[1].wait()
    copies[2].wait()


def block_bias(place, lower):
    return jnp.where(place >= lower, 0.0, NEG)


def attend_pairs(q_ref, block_ref, n, bias_ref, s_refs, p_refs, carry_in, finish):
    scale = HEAD_DIM ** (-0.5) * LOG2E
    wide = n * ROWS
    chunk = 32
    ones = jnp.ones((wide, 128), BF16)

    def group(g, carry):
        at = pl.multiple_of(g * 128, 128)
        keys = block_ref[:, :, pl.ds(at, 128)].reshape(wide, 128)
        for half in range(2):
            from_col = pl.multiple_of(g * 512 + half * 256, 256)
            both = q_ref[:, pl.ds(from_col, 256)]
            q = jnp.concatenate([both[:, :128], both[:, 128:]], axis=0)
            s_refs[half][...] = lax.dot_general(
                q, keys, (((1,), (1,)), ((), ())), preferred_element_type=F32
            )
        values = block_ref[:, :, pl.ds(pl.multiple_of(at + 256, 128), 128)].reshape(wide, 128)
        values = jnp.concatenate([values, ones], axis=1)
        for half in range(2):
            index = 2 * g + half
            for c in range(2 * ROWS // chunk):
                rows = slice(c * chunk, (c + 1) * chunk)
                from_row = (c * chunk) % ROWS
                s = s_refs[half][rows] * scale + bias_ref[from_row : from_row + chunk]
                top = jnp.max(s, axis=-1, keepdims=True)
                if carry_in is not None:
                    before = carry_in[3][index, rows]
                    top = jnp.maximum(top, before)
                    alpha = jnp.exp2(before - top)
                    carry_in[0][index, rows] = alpha
                    top = top[:, :1]
                p_refs[half][rows] = jnp.exp2(s - top).astype(BF16)
                if carry_in is None:
                    finish[0][index, rows] = jnp.broadcast_to(top, (chunk, 128))
            both = jnp.dot(p_refs[half][...], values, preferred_element_type=F32)
            blended, total = both[:, :128], both[:, 128:]
            if carry_in is None:
                finish[1][index] = total
                finish[2][index] = blended
            else:
                alpha = carry_in[0][index]
                total = total + alpha * carry_in[1][index]
                blended = ((blended + alpha * carry_in[2][index]) / total).astype(BF16)
                finish[:, pl.ds(pl.multiple_of(index * 256, 256), 256)] = jnp.concatenate(
                    [blended[:ROWS], blended[ROWS:]], axis=1
                )
        return carry

    lax.fori_loop(0, 2, group, 0)


def attend_scratch(n, extra=()):
    return [
        pltpu.VMEM((ROWS, n * ROWS), F32),
        pltpu.VMEM((n, ROWS, 512), BF16),
        pltpu.VMEM((ROWS, 1024), BF16),
        pltpu.VMEM((2 * ROWS, n * ROWS), F32),
        pltpu.VMEM((2 * ROWS, n * ROWS), F32),
        pltpu.VMEM((2 * ROWS, n * ROWS), BF16),
        pltpu.VMEM((2 * ROWS, n * ROWS), BF16),
        *extra,
        pltpu.SemaphoreType.DMA((n + 1,)),
    ]


def attend_first_kernel(
    info_ref, q_hbm, own_ref, y1_hbm, y2_hbm, weight_hbm,
    top_ref, total_ref, sum_ref, weight_ref,
    bias_ref, block_ref, q_ref, s0, s1, e0, e1, weight_sem, sem,
):
    copies = [fetch(q_hbm, q_ref, sem.at[3])]
    for k, source in enumerate((own_ref, y1_hbm, y2_hbm)):
        copies.append(fetch(source, block_ref.at[k], sem.at[k]))
    row = lax.broadcasted_iota(jnp.int32, (ROWS, ROWS), 0)
    col = lax.broadcasted_iota(jnp.int32, (ROWS, ROWS), 1)
    lower = jnp.maximum(first_token(info_ref, row), row - (WINDOW - 1))
    bias_ref[:, :ROWS] = jnp.where((col >= lower) & (col <= row), 0.0, NEG)
    bias_ref[:, ROWS : 2 * ROWS] = block_bias(col - 4 * ROWS, lower)
    bias_ref[:, 2 * ROWS :] = block_bias(col - 8 * ROWS, lower)
    for copy in copies:
        copy.wait()
    weight = fetch(weight_hbm, weight_ref, weight_sem)
    attend_pairs(q_ref, block_ref, 3, bias_ref, (s0, s1), (e0, e1), None, (top_ref, total_ref, sum_ref))
    weight.wait()


def attend_rest_kernel(
    info_ref, q_hbm, p1, p2, p3, w1, w2, w3, r1, r2, r3, top_ref, total_ref, sum_ref, other_hbm, own_hbm,
    out_ref, other_ref, own_ref,
    bias_ref, block_ref, q_ref, s0, s1, e0, e1, alpha_ref, weight_sem, sem,
):
    z = info_ref[4]
    copies = [fetch(q_hbm, q_ref, sem.at[6])]
    for s, (p, w) in enumerate(((p1, w1), (p2, w2), (p3, w3))):

        @pl.when(z >= s + 1)
        def _():
            pltpu.make_async_copy(p, block_ref.at[s], sem.at[s]).start()

        @pl.when(z < s + 1)
        def _():
            pltpu.make_async_copy(w, block_ref.at[s], sem.at[s]).start()

    for s, r in enumerate((r1, r2, r3)):
        copies.append(fetch(r, block_ref.at[3 + s], sem.at[3 + s]))
    row = lax.broadcasted_iota(jnp.int32, (ROWS, 1), 0)
    col = lax.broadcasted_iota(jnp.int32, (ROWS, ROWS), 1)
    lower = jnp.maximum(first_token(info_ref, row), row - (WINDOW - 1))
    for s in range(3):
        near = z >= s + 1
        bias_ref[:, s * ROWS : (s + 1) * ROWS] = block_bias(col - jnp.where(near, s + 1, s + 5) * ROWS, lower)
        bias_ref[:, (s + 3) * ROWS : (s + 4) * ROWS] = block_bias(
            col - jnp.where(near, s + 5, s + 1) * ROWS, lower
        )
    for copy in copies:
        copy.wait()
    for s in range(3):
        pltpu.make_async_copy(p1, block_ref.at[s], sem.at[s]).wait()
    weights = [
        fetch(own_hbm, own_ref, weight_sem.at[0]),
        fetch(other_hbm, other_ref, weight_sem.at[1]),
    ]
    attend_pairs(
        q_ref, block_ref, 6, bias_ref, (s0, s1), (e0, e1), (alpha_ref, total_ref, sum_ref, top_ref), out_ref
    )
    for weight in weights:
        weight.wait()


def attend(info, queries, own, inner_weight, own_weight, other_weight):
    near = range(4)
    y1 = moved(own, [(4 * y + x, 4 * y + 4 + x) for y in range(3) for x in near])
    y2 = moved(own, [(4 * y + x, 4 * y + 8 + x) for y in range(2) for x in near])
    p = [moved(own, [(4 * y + x, 4 * y + x + s) for y in near for x in near if x + s < 4]) for s in (1, 2, 3)]
    r = [moved(y1, [(4 * y + x, 4 * y + (x + s) % 4) for y in (1, 2, 3) for x in near]) for s in (1, 2, 3)]
    p[1] = moved(own, [(4 * y + x, 4 * y + (x + 2) % 4) for y in near for x in near])
    r[1] = moved(p[1], [(4 * y + x, 4 * y + 4 + x) for y in range(3) for x in near])
    w = [moved(y2, [(4 * y + x, 4 * y + x + s - 4) for y in (2, 3) for x in near if x + s >= 4]) for s in (1, 2, 3)]
    part = ("v", (4, 2 * ROWS, 128), F32)
    one = pltpu.SemaphoreType.DMA
    *carry, inner_near = call(
        attend_first_kernel,
        [part] * 3 + [("v", (2048, 2048), BF16)],
        "shaaah",
        attend_scratch(3, [one]),
        20,
        1_600_000_000,
        4 << 20,
    )(info, queries, own, y1, y2, inner_weight)
    attended, other_near, own_near = call(
        attend_rest_kernel,
        [("v", (ROWS, 1024), BF16), ("v", (1024, 2048), BF16), ("v", (1024, 2048), BF16)],
        "sh" + "a" * 9 + "vvvah",
        attend_scratch(6, [pltpu.VMEM((4, 2 * ROWS, 128), F32), pltpu.SemaphoreType.DMA((2,))]),
        32,
        3_400_000_000,
        4 << 20,
    )(info, queries, *p, *w, *r, *carry, other_weight, own_weight)
    return attended, inner_near, own_near, other_near


def own_part_kernel(x_ref, w_ref, out_ref):
    for n in range(4):
        cols = slice(n * 512, n * 512 + 512)
        out_ref[:, cols] = jnp.dot(x_ref[...], w_ref[:, cols], preferred_element_type=F32)


def token_kernel(
    x_ref, w_ref, mine_ref, hidden_hbm, gain_ref, inner_ref, state_hbm, step_ref,
    residual_hbm, normed_hbm, raw_ref, state_out_ref, step_out_ref, rim_ref,
    hidden_ref, state_ref, theirs_ref, residual_ref, normed_ref, sem,
):
    hidden = fetch(hidden_hbm, hidden_ref, sem.at[0])
    state = fetch(state_hbm, state_ref, sem.at[1])
    theirs_ref[:, :512] = jnp.dot(x_ref[...], w_ref[:, :512], preferred_element_type=F32)
    hidden.wait()
    squares = jnp.zeros((ROWS, 128), F32)
    for n in range(4):
        cols = slice(n * 512, n * 512 + 512)
        if n > 0:
            theirs_ref[:, cols] = jnp.dot(x_ref[...], w_ref[:, cols], preferred_element_type=F32)
        total = hidden_ref[:, cols].astype(F32) + (mine_ref[:, cols] + theirs_ref[:, cols])
        low = total.astype(BF16)
        residual_ref[:, cols] = low
        wide = low.astype(F32)
        wide = wide * wide
        squares = squares + (wide[:, :128] + wide[:, 128:256]) + (wide[:, 256:384] + wide[:, 384:])
    residual = fetch(residual_ref, residual_hbm, sem.at[2])
    mean = jnp.sum(squares, axis=-1, keepdims=True) * (1.0 / 2048.0)
    scale = lax.rsqrt(mean + EPSILON)
    for n in range(4):
        cols = slice(n * 512, (n + 1) * 512)
        normed_ref[:, cols] = (
            residual_ref[:, cols].astype(F32) * scale * gain_ref[:, cols].astype(F32)
        ).astype(BF16)
    normed = fetch(normed_ref, normed_hbm, sem.at[3])
    state.wait()
    narrow = jnp.dot(normed_ref[...], state_ref[...], preferred_element_type=F32).astype(BF16)
    state_out_ref[...] = narrow
    rim_ref[:, 2048:] = narrow[ROWS - 8 :]
    step_out_ref[...] = lax.dot_general(
        normed_ref[...], step_ref[...], (((1,), (1,)), ((), ())), preferred_element_type=F32
    )

    def in_tile(n, carry):
        cols = columns(n)
        raw = jnp.dot(normed_ref[...], inner_ref[:, cols], preferred_element_type=F32).astype(BF16)
        raw_ref[:, cols] = raw
        rim_ref[:, cols] = raw[ROWS - 8 :]
        return carry

    lax.fori_loop(0, 4, in_tile, 0)
    residual.wait()
    normed.wait()


def gate_kernel(x_hbm, w_hbm, after_ref, out_ref, x_ref, w_ref, sem):
    first = fetch(x_hbm, x_ref, sem.at[4])
    for n in range(4):
        fetch(w_hbm.at[:, n * 512 : n * 512 + 512], w_ref.at[:, n * 512 : n * 512 + 512], sem.at[n])
    first.wait()

    def tile(n, carry):
        cols = columns(n)
        pltpu.make_async_copy(w_hbm.at[:, cols], w_ref.at[:, cols], sem.at[n]).wait()
        out_ref[:, cols] = jnp.dot(x_ref[...], w_ref[:, cols], preferred_element_type=F32).astype(BF16)
        return carry

    lax.fori_loop(0, 4, tile, 0)


def scale_kernel(gated_ref, mine_ref, theirs_ref, gain_ref, out_ref):
    squares = jnp.broadcast_to(mine_ref[...] + theirs_ref[...], (128, ROWS))
    scale = lax.rsqrt(jnp.transpose(squares) * (1.0 / D_INNER) + EPSILON)
    for j in range(CONTEXT):
        cols = slice(j * PIECE, (j + 1) * PIECE)
        out_ref[:, cols] = (gated_ref[:, cols] * scale * gain_ref[:, cols].astype(F32)).astype(BF16)


def conv_sum(raw, taps, moves):
    taps = taps.astype(F32)
    total = raw.astype(F32) * taps[CONV - 1 : CONV]
    for back in range(1, CONV):
        tap = taps[CONV - 1 - back : CONV - back]
        total = total + jnp.dot(moves[back - 1], raw, preferred_element_type=F32) * tap
    return total


def conv_edge(rim, taps, start, row):
    early = rim.astype(F32)
    taps = taps.astype(F32)
    edge = jnp.zeros_like(early)
    for back in range(1, CONV):
        tap = taps[CONV - 1 - back : CONV - back]
        keep = (row < back) & (row - back >= start)
        edge = edge + jnp.where(keep, pltpu.roll(early, back, 0) * tap, 0.0)
    return edge


def silu(x):
    return x * jax.nn.sigmoid(x)


def spread_pair(values, j, lane):
    return jnp.where(lane < 64, values[:, 2 * j : 2 * j + 1], values[:, 2 * j + 1 : 2 * j + 2])


def prepare_kernel(
    info_ref, raw_ref, state_ref, step_raw_ref, bias_ref, decay_ref, taps_ref, state_taps_ref,
    inner_hbm, reads_hbm, running_hbm, rows_hbm, piece_ref, decays_ref, head_ref, tail_ref,
    inner_ref, reads_ref, running_ref, rows_ref, moves_ref, sem,
):
    row = lax.broadcasted_iota(jnp.int32, (ROWS, 1), 0)
    wide_row = lax.broadcasted_iota(jnp.int32, (ROWS, ROWS), 0)
    col = lax.broadcasted_iota(jnp.int32, (ROWS, ROWS), 1)
    lane = lax.broadcasted_iota(jnp.int32, (ROWS, PIECE), 1)
    start = first_token(info_ref, wide_row)
    for back in range(1, CONV):
        chosen = (col == wide_row - back) & (col >= start)
        moves_ref[back - 1] = jnp.where(chosen, 1.0, 0.0).astype(BF16)
    moves = [moves_ref[k] for k in range(CONV - 1)]
    total = conv_sum(state_ref[...], state_taps_ref[...], moves)
    head_ref[:, 2048:] = total[:HEAD]
    state = silu(total).astype(BF16)
    read_in = state[:, :STATE]
    reads_ref[0] = read_in
    reads_ref[1] = state[:, STATE:]
    step = jax.nn.softplus(step_raw_ref[...] + bias_ref[...])
    running = -jnp.exp(decay_ref[...]) * step
    reach = 1
    while reach < ROWS:
        running = running + jnp.where(row >= reach, pltpu.roll(running, reach, 0), 0.0)
        reach *= 2
    running_ref[...] = running
    rows_ref[0] = jnp.transpose(running)
    rows_ref[1] = jnp.transpose(step)
    copies = [
        fetch(reads_ref, reads_hbm, sem.at[0]),
        fetch(running_ref, running_hbm, sem.at[1]),
        fetch(rows_ref, rows_hbm, sem.at[2]),
    ]
    last = running[ROWS - 1 :]
    last_start = start[ROWS - 1 :, :1]
    tail = jnp.where(row >= last_start, jnp.exp(last - running), 0.0) * step
    final = jnp.where(last_start < 0, jnp.exp(last), 0.0)
    final = jnp.broadcast_to(final, (16, final.shape[1]))
    line = lax.broadcasted_iota(jnp.int32, (16, PIECE), 0)
    for n in range(8):
        cols = slice(n * 256, (n + 1) * 256)
        total = conv_sum(raw_ref[:, cols], taps_ref[:, cols], moves)
        head_ref[:, cols] = total[:HEAD]
        inner_ref[:, cols] = silu(total).astype(BF16)
        if n % 2 == 1:
            group = slice((n - 1) * 256, (n + 1) * 256)
            copies.append(fetch(inner_ref.at[:, group], inner_hbm.at[:, group], sem.at[3 + n // 2]))
    late = jnp.where(row >= HEAD, tail, 0.0)
    for j in range(CONTEXT):
        cols = slice(j * PIECE, (j + 1) * PIECE)
        tail_ref[:, cols] = spread_pair(tail[:HEAD], j, lane[:HEAD])
        weighted = (spread_pair(late, j, lane) * inner_ref[:, cols].astype(F32)).astype(BF16)
        piece_ref[j] = lax.dot_general(
            read_in, weighted, (((0,), (0,)), ((), ())), preferred_element_type=F32
        )
        decay = spread_pair(final, j, lane[:16])
        high = decay.astype(BF16).astype(F32)
        decays_ref[j] = jnp.where(line == 0, high, decay - high).astype(BF16)
    for copy in copies:
        copy.wait()


def edge_kernel(
    info_ref, rim_ref, head_ref, tail_ref, part_ref, decays_ref, taps_ref, state_taps_ref,
    inner_ref, reads_ref, piece_ref,
):
    row = lax.broadcasted_iota(jnp.int32, (8, 1), 0)
    start = first_token(info_ref, row)
    rest = jnp.zeros((HEAD - 8, 2304), F32)
    edge = jnp.concatenate(
        [
            conv_edge(rim_ref[:, :2048], taps_ref[...], start, row),
            conv_edge(rim_ref[:, 2048:], state_taps_ref[...], start, row),
        ],
        axis=1,
    )
    full = silu(head_ref[...] + jnp.concatenate([edge, rest], axis=0)).astype(BF16)
    inner = full[:, :2048]
    inner_ref[...] = inner
    reads_ref[0] = full[:, 2048 : 2048 + STATE]
    reads_ref[1] = full[:, 2048 + STATE :]
    weighted = (tail_ref[...] * inner.astype(F32)).astype(BF16)
    more = lax.dot_general(
        full[:, 2048 : 2048 + STATE], weighted, (((0,), (0,)), ((), ())), preferred_element_type=F32
    )
    for j in range(CONTEXT):
        piece = part_ref[j] + more[:, j * PIECE : (j + 1) * PIECE]
        piece_ref[j, :STATE] = piece.astype(BF16)
        piece_ref[j, STATE:] = decays_ref[j]


def within_kernel(
    info_ref, inner_hbm, reads_hbm, running_hbm, rows_hbm, inner_head_hbm, reads_head_hbm, skip_ref, within_ref,
    inner_ref, reads_ref, running_ref, rows_ref, sem,
):
    copies = [
        fetch(reads_hbm.at[:, HEAD:], reads_ref.at[:, HEAD:], sem.at[0]),
        fetch(running_hbm, running_ref, sem.at[1]),
        fetch(rows_hbm, rows_ref, sem.at[2]),
        fetch(inner_hbm.at[HEAD:], inner_ref.at[HEAD:], sem.at[3]),
        fetch(reads_head_hbm, reads_ref.at[:, :HEAD], sem.at[4]),
        fetch(inner_head_hbm, inner_ref.at[:HEAD], sem.at[5]),
    ]
    row = lax.broadcasted_iota(jnp.int32, (ROWS, ROWS), 0)
    col = lax.broadcasted_iota(jnp.int32, (ROWS, ROWS), 1)
    same = (col >= first_token(info_ref, row)) & (col <= row)
    lane = lax.broadcasted_iota(jnp.int32, (ROWS, PIECE), 1)
    for copy in copies:
        copy.wait()
    pairwise = lax.dot_general(
        reads_ref[1], reads_ref[0], (((1,), (1,)), ((), ())), preferred_element_type=F32
    )
    pairwise = jnp.where(same, pairwise, 0.0)
    for j in range(CONTEXT):
        cols = slice(j * PIECE, (j + 1) * PIECE)
        inner = inner_ref[:, cols]
        parts = []
        for half in range(2):
            h = 2 * j + half
            gap = running_ref[:, h : h + 1] - rows_ref[0, h : h + 1, :]
            decay = jnp.exp(jnp.minimum(gap, 0.0))
            mixing = (decay * pairwise * rows_ref[1, h : h + 1, :]).astype(BF16)
            parts.append(jnp.dot(mixing, inner, preferred_element_type=F32))
        both = jnp.where(lane < 64, parts[0], parts[1])
        within_ref[:, cols] = both + skip_ref[:, cols] * inner.astype(F32)


def scan_kernel(piece_ref, after_ref, out_ref):
    carried = jnp.zeros((STATE, PIECE), F32)
    for k in range(CONTEXT):
        out_ref[k] = carried.astype(BF16)
        decay = piece_ref[k, STATE : STATE + 1, :].astype(F32) + piece_ref[k, STATE + 1 : STATE + 2, :].astype(F32)
        carried = decay * carried + piece_ref[k, :STATE, :].astype(F32)


def finish_kernel(
    info_ref, within_ref, gate_ref, reads_hbm, reads_head_hbm, running_hbm, carried_hbm, gated_ref, square_ref,
    read_ref, running_ref, carried_ref, sem,
):
    copies = [
        fetch(running_hbm, running_ref, sem.at[0]),
        fetch(reads_hbm.at[1, HEAD:], read_ref.at[HEAD:], sem.at[1]),
        fetch(reads_head_hbm.at[1], read_ref.at[:HEAD], sem.at[3]),
    ]
    copies.append(fetch(carried_hbm, carried_ref, sem.at[2]))
    row = lax.broadcasted_iota(jnp.int32, (ROWS, 1), 0)
    lane = lax.broadcasted_iota(jnp.int32, (ROWS, PIECE), 1)
    open_row = first_token(info_ref, row) < 0
    for copy in copies:
        copy.wait()
    entry = jnp.where(open_row, jnp.exp(running_ref[...]), 0.0)
    read_out = read_ref[...]
    squares = jnp.zeros((ROWS, PIECE), F32)
    for j in range(CONTEXT):
        cols = slice(j * PIECE, (j + 1) * PIECE)
        carried = jnp.dot(read_out, carried_ref[j], preferred_element_type=F32)
        ssm = within_ref[:, cols] + carried * spread_pair(entry, j, lane)
        gate = gate_ref[:, cols].astype(F32)
        gated = ssm * (gate * jax.nn.sigmoid(gate))
        gated_ref[:, cols] = gated
        squares = squares + gated * gated
    square_ref[...] = jnp.sum(jnp.transpose(squares), axis=0, keepdims=True)


def per_device(
    queries,
    key_states,
    value_states,
    segment_ids,
    hidden,
    attn_out_weight,
    norm_gain,
    gate_weight,
    inner_weight,
    state_proj_weight,
    step_weight,
    conv_inner,
    conv_state,
    step_bias,
    decay_log,
    skip_gain,
    out_gain,
):
    heads = step_weight.shape[1]
    dma = pltpu.SemaphoreType.DMA
    own, info = call(
        pack_kernel,
        [("v", (ROWS, 512), BF16), ("s", (8,), jnp.int32)],
        "hhh",
        [pltpu.VMEM((32, 128), jnp.int32), dma((3,))],
        4,
    )(key_states, value_states, segment_ids.reshape(32, 128))
    other_weight = swapped(attn_out_weight)
    attended, inner_near, own_near, other_near = attend(
        info, queries, own, inner_weight, attn_out_weight, other_weight
    )
    other = swapped(attended)
    mine = call(
        own_part_kernel, [("v", (ROWS, 2048), F32)], "vv", (), 8, 1_100_000_000, 4 << 20
    )(attended, own_near)
    residual, normed, inner_raw, state_raw, step_raw, rim = call(
        token_kernel,
        [
            ("h", (ROWS, 2048), BF16),
            ("h", (ROWS, 2048), BF16),
            ("v", (ROWS, 2048), BF16),
            ("v", (ROWS, 256), BF16),
            ("v", (ROWS, heads), F32),
            ("v", (8, 2304), BF16),
        ],
        "vvvhvvhv",
        [
            pltpu.VMEM((ROWS, 2048), BF16),
            pltpu.VMEM((2048, 256), BF16),
            pltpu.VMEM((ROWS, 2048), F32),
            pltpu.VMEM((ROWS, 2048), BF16),
            pltpu.VMEM((ROWS, 2048), BF16),
            dma((4,)),
        ],
        16,
        3_600_000_000,
        14 << 20,
    )(other, other_near, mine, hidden, norm_gain[None, :], inner_near, state_proj_weight, step_weight.T)
    rim = moved(rim, [(i, i + 1) for i in range(CONTEXT - 1)])
    buffers = [
        pltpu.VMEM((ROWS, 2048), BF16),
        pltpu.VMEM((2, ROWS, STATE), BF16),
        pltpu.VMEM((ROWS, heads), F32),
        pltpu.VMEM((2, heads, ROWS), F32),
    ]
    inner, reads, running, rows, part, decays, head, tail = call(
        prepare_kernel,
        [
            ("h", (ROWS, 2048), BF16),
            ("h", (2, ROWS, STATE), BF16),
            ("h", (ROWS, heads), F32),
            ("h", (2, heads, ROWS), F32),
            ("v", (CONTEXT, STATE, PIECE), F32),
            ("v", (CONTEXT, 16, PIECE), BF16),
            ("v", (HEAD, 2304), F32),
            ("v", (HEAD, 2048), F32),
        ],
        "svvvvvvv",
        buffers + [pltpu.VMEM((CONV - 1, ROWS, ROWS), BF16), dma((7,))],
        16,
        1_000_000_000,
        3 << 20,
    )(info, inner_raw, state_raw, step_raw, step_bias[None, :], decay_log[None, :], conv_inner, conv_state)
    inner_head, reads_head, pieces = call(
        edge_kernel,
        [
            ("v", (HEAD, 2048), BF16),
            ("v", (2, HEAD, STATE), BF16),
            ("v", (CONTEXT, PIECE_ROWS, PIECE), BF16),
        ],
        "svvvvvvv",
        (),
        8,
        10_000_000,
        2 << 20,
    )(info, rim, head, tail, part, decays, conv_inner, conv_state)
    gathered = lax.all_to_all(pieces, "context", 0, 0, tiled=True)
    skip = jnp.repeat(skip_gain, 64)[None, :]
    within = call(
        within_kernel,
        [("v", (ROWS, 2048), F32)],
        "shhhhaav",
        buffers + [dma((6,))],
        16,
        3_000_000_000,
        4 << 20,
    )(info, inner, reads, running, rows, inner_head, reads_head, skip)
    carried = call(
        scan_kernel, [("v", (CONTEXT, STATE, PIECE), BF16)], "va", (), 8, 1_000_000, 1 << 20
    )(gathered, within)
    gate = call(
        gate_kernel,
        [("v", (ROWS, 2048), BF16)],
        "hha",
        [pltpu.VMEM((ROWS, 2048), BF16), pltpu.VMEM((2048, 2048), BF16), dma((5,))],
        20,
        2_200_000_000,
        9 << 20,
    )(normed, gate_weight, carried)
    carried = lax.all_to_all(carried, "context", 0, 0, tiled=True)
    gated, squares = call(
        finish_kernel,
        [("v", (ROWS, 2048), F32), ("v", (1, ROWS), F32)],
        "svvhaha",
        [
            pltpu.VMEM((ROWS, STATE), BF16),
            pltpu.VMEM((ROWS, heads), F32),
            pltpu.VMEM((CONTEXT, STATE, PIECE), BF16),
            dma((4,)),
        ],
        16,
        1_000_000_000,
        6 << 20,
    )(info, within, gate, reads, reads_head, running, carried)
    mixed = call(
        scale_kernel, [("v", (ROWS, 2048), BF16)], "vvvv", (), 8, 2_000_000, 3 << 20
    )(gated, squares, swapped(squares), out_gain[None, :])
    return (residual, mixed)


def solution(mesh):
    in_specs = (
        P(("seq", "context"), "tensor"),
        P(("seq", "context"), "tensor"),
        P(("seq", "context"), "tensor"),
        P("seq"),
        P(("seq", "context"), None),
        P("tensor", None),
        P(),
        P(None, "tensor"),
        P(None, "tensor"),
        P(),
        P(None, "tensor"),
        P(None, "tensor"),
        P(),
        P("tensor"),
        P("tensor"),
        P("tensor"),
        P("tensor"),
    )
    out_specs = (P(("seq", "context"), None), P(("seq", "context"), "tensor"))
    return jax.shard_map(
        per_device, mesh=mesh, in_specs=in_specs, out_specs=out_specs, check_vma=False
    )
```
